256 devices in a mesh: row: 16 (over y, z_hi, core), col: 16 (over z_lo, x).
Axes of the slice: x: 4, y: 4, z: 8 (z_hi: 2, z_lo: 4; z = z_hi * 4 + z_lo), core: 2. Of those that a mesh axis runs over, the one named last changes fastest.
Arguments:
- object_field: float32 [2, 4096, 4096], P(None, 'row', 'col'), may hold values from -4 to 4
- modes: bfloat16 [16, 12, 2, 256, 256], P('row', None, None, 'col'), may hold values from -5 to 5
- coeffs: float32 [16, 16, 4, 12], P('row', 'col'), may hold values from -1.5 to 1.5
- offsets: int32 [16, 16, 4, 2], P('row', 'col'), may hold values from -128 to 128, as said below
- region: int32 [16, 16, 4], P('row', 'col'), may hold values from 0 to 15, as said below
- counts: int32 [16, 16], P('row', 'col'), may hold values from 1 to 4, as said below
- intensity: bfloat16 [16, 16, 4, 256, 256], P('row', 'col'), may hold values from 0.049804688 to 4
Outputs:
- object_grad: float32 [2, 4096, 4096], P(None, 'row', 'col')
- mode_grad: float32 [16, 12, 2, 256, 256], P('row', None, None, 'col')
The draws below stay inside these ranges and needn't reach their ends.
Inputs may be any that keep to these rules, and one draw needn't show every extreme that they name: `offsets`: every window reaches at most 128 cells beyond its tile on each side; every tile has a live slot whose window starts at row offset -128 and column offset 256 - 256 / 2. A position's region is its tile's row index or the next one; slot 0 of every tile has its own row's region. Slots 0 to counts - 1 of a tile are live, the rest are ignored; some tile is full and some tile has one live slot.
All inputs are finite; a program needn't handle non-finite values.
Results may differ from the reference program's by a relative error of at most 0.014.
Values may be sent and summed in bfloat16 or wider, within the bound.
A program may use at most 64 MiB of HBM per device.

```python
import math
import jax
import jax.numpy as jnp
from jax import lax

W = 256
K = 12
TILE = 256
P_DEV = 4
REGIONS = 16
TILE_COLS = 16
NY = 4096
NX = 4096


def common_counts(key):
    base_key = jax.random.fold_in(key, 101)
    tile_total = REGIONS * TILE_COLS
    counts = jax.random.randint(base_key, (tile_total,), 1, P_DEV + 1)
    full_tile = jax.random.randint(jax.random.fold_in(base_key, 1), (), 0, tile_total)
    tile_gap = jax.random.randint(jax.random.fold_in(base_key, 2), (), 1, tile_total)
    single_tile = (full_tile + tile_gap) % tile_total
    counts = counts.at[full_tile].set(P_DEV).at[single_tile].set(1)
    return counts.reshape(REGIONS, TILE_COLS).astype(jnp.int32)


def draw_counts(key, part):
    return common_counts(key)


def draw_offsets(key, part):
    counts = common_counts(key)
    half_size = W // 2
    corners = jax.random.randint(jax.random.fold_in(key, 202), (REGIONS, TILE_COLS, P_DEV, 2), -half_size, TILE - half_size + 1)
    picks = jax.random.randint(jax.random.fold_in(key, 203), (REGIONS, TILE_COLS), 0, 1 << 20) % counts
    chosen = jnp.arange(P_DEV, dtype=jnp.int32)[None, None, :] == picks[:, :, None]
    top_side = jnp.where(chosen, -half_size, corners[..., 0])
    left_side = jnp.where(chosen, TILE - half_size, corners[..., 1])
    return jnp.stack([top_side, left_side], axis=-1).astype(jnp.int32)


def draw_region(key, part):
    steps_up = jax.random.randint(jax.random.fold_in(key, 303), (REGIONS, TILE_COLS, P_DEV), 0, 2)
    steps_up = steps_up.at[:, :, 0].set(0)
    row_ids = jnp.arange(REGIONS, dtype=jnp.int32)[:, None, None]
    return jnp.minimum(row_ids + steps_up, REGIONS - 1).astype(jnp.int32)


def levels(rng, dims, pieces, smallest, largest):
    factor_of = 1.0
    for axis_at, parts in pieces:
        draws = jax.random.uniform(jax.random.fold_in(jax.random.fold_in(rng, 6), axis_at), (parts,), jnp.float32, smallest / len(pieces), largest / len(pieces))
        factor_of = factor_of * jnp.repeat(jnp.exp(draws), dims[axis_at] // parts).reshape((-1,) + (1,) * (len(dims) - 1 - axis_at))
    return factor_of


def bell_draw(stream_key, dims, scale, bound, cuts=(), kind=jnp.bfloat16):
    gain = levels(stream_key, dims, cuts, -0.22, 0.18) if cuts else 1.0
    result = jax.random.normal(stream_key, dims, jnp.float32) * scale * gain
    return jnp.minimum(jnp.maximum(result, -bound), bound).astype(kind)


def setup_inputs(seed: int = 0) -> dict:
    keys = jax.random.split(jax.random.key(seed), 8)
    return {
        "object_field": bell_draw(keys[0], (2, NY, NX), 0.7, 4.0, ((1, 16), (2, 16)), jnp.float32),
        "modes": bell_draw(keys[1], (REGIONS, K, 2, W, W), 1.0, 5.0, ((0, 16), (3, 16))),
        "coeffs": bell_draw(keys[2], (REGIONS, TILE_COLS, P_DEV, K), 0.3, 1.5, ((0, 16), (1, 16)), jnp.float32),
        "offsets": draw_offsets(jax.random.fold_in(keys[7], 71), 0),
        "region": draw_region(jax.random.fold_in(keys[7], 71), 0),
        "counts": draw_counts(jax.random.fold_in(keys[7], 71), 0),
        "intensity": jnp.clip(jnp.exp(math.log(4.0) - 4.3859405 * jax.random.uniform(keys[6], (REGIONS, TILE_COLS, P_DEV, W, W), jnp.float32) ** levels(keys[6], (REGIONS, TILE_COLS, P_DEV, W, W), ((0, 16), (1, 16)), -0.2, 0.2)), 0.049804688, 4.0).astype(jnp.bfloat16),
    }


FLOOR = 0.25

def dft_tables(length):
    indices = jnp.arange(length, dtype=jnp.int32)
    phases = indices[:, None] * indices[None, :] % length
    angles = phases.astype(jnp.float32) * (2.0 * math.pi / length)
    scaling = 1.0 / math.sqrt(length)
    return ((jnp.cos(angles) * scaling).astype(jnp.bfloat16), (-jnp.sin(angles) * scaling).astype(jnp.bfloat16))

def left_apply(table_re, table_im, real_part, imag_part, orient):

    def multiply(table, operand):
        return jnp.einsum('mr,prn->pmn', table.astype(jnp.float32), operand.astype(jnp.float32), precision=lax.Precision.HIGHEST)
    out_re = multiply(table_re, real_part) - orient * multiply(table_im, imag_part)
    out_im = multiply(table_re, imag_part) + orient * multiply(table_im, real_part)
    return (out_re, out_im)

def right_apply(table_re, table_im, real_part, imag_part, orient):

    def multiply(operand, table):
        return jnp.einsum('pmc,cn->pmn', operand.astype(jnp.float32), table.astype(jnp.float32), precision=lax.Precision.HIGHEST)
    out_re = multiply(real_part, table_re) - orient * multiply(imag_part, table_im)
    out_im = multiply(imag_part, table_re) + orient * multiply(real_part, table_im)
    return (out_re, out_im)

def reference(object_field, modes, coeffs, offsets, region, counts, intensity):
    half_size = W // 2
    table_re, table_im = dft_tables(W)
    padded = jnp.pad(object_field.astype(jnp.bfloat16), ((0, 0), (half_size, half_size), (half_size, half_size)))
    grad_init = jnp.zeros(padded.shape, jnp.float32)
    modes_init = jnp.zeros(modes.shape, jnp.float32)

    def tile_step(carry, tile_id):
        grad_acc, mode_acc = carry
        row_id = tile_id // TILE_COLS
        col_id = tile_id % TILE_COLS
        next_row = jnp.minimum(row_id + 1, REGIONS - 1)
        weights = coeffs[row_id, col_id]
        regions = region[row_id, col_id]
        corners = offsets[row_id, col_id]
        own_mask = (regions == row_id).astype(jnp.float32)
        next_mask = (regions == row_id + 1).astype(jnp.float32)
        mixing = jnp.concatenate([weights * own_mask[:, None], weights * next_mask[:, None]], axis=1)
        stacked = jnp.concatenate([modes[row_id], modes[next_row]], axis=0).astype(jnp.float32).reshape(2 * K, -1)
        probes = jnp.dot(mixing, stacked, precision=lax.Precision.HIGHEST).reshape(P_DEV, 2, W, W).astype(jnp.bfloat16)
        base_row = row_id * TILE
        base_col = col_id * TILE

        def cut_window(corner):
            return lax.dynamic_slice(padded, (jnp.int32(0), base_row + corner[0] + half_size, base_col + corner[1] + half_size), (2, W, W))
        windows = jax.vmap(cut_window)(corners)
        probe_re = probes[:, 0].astype(jnp.float32)
        probe_im = probes[:, 1].astype(jnp.float32)
        window_re = windows[:, 0].astype(jnp.float32)
        window_im = windows[:, 1].astype(jnp.float32)
        exit_re = (probe_re * window_re - probe_im * window_im).astype(jnp.bfloat16)
        exit_im = (probe_re * window_im + probe_im * window_re).astype(jnp.bfloat16)
        half_re, half_im = left_apply(table_re, table_im, exit_re, exit_im, 1.0)
        far_re, far_im = right_apply(table_re, table_im, half_re.astype(jnp.bfloat16), half_im.astype(jnp.bfloat16), 1.0)
        magnitude = jnp.sqrt(far_re * far_re + far_im * far_im)
        measured = jnp.sqrt(intensity[row_id, col_id].astype(jnp.float32))
        live = (jnp.arange(P_DEV, dtype=jnp.int32) < counts[row_id, col_id]).astype(jnp.float32)
        factor = (measured / jnp.maximum(magnitude, FLOOR) - 1.0) * live[:, None, None]
        change_re = (far_re * factor).astype(jnp.bfloat16)
        change_im = (far_im * factor).astype(jnp.bfloat16)
        back_re, back_im = left_apply(table_re, table_im, change_re, change_im, -1.0)
        update_re, update_im = right_apply(table_re, table_im, back_re.astype(jnp.bfloat16), back_im.astype(jnp.bfloat16), -1.0)
        object_terms = jnp.stack([probe_re * update_re + probe_im * update_im, probe_re * update_im - probe_im * update_re], axis=1)

        def place(position, accum):
            start_row = base_row + corners[position, 0] + half_size
            start_col = base_col + corners[position, 1] + half_size
            current = lax.dynamic_slice(accum, (jnp.int32(0), start_row, start_col), (2, W, W))
            return lax.dynamic_update_slice(accum, current + object_terms[position], (jnp.int32(0), start_row, start_col))
        grad_acc = lax.fori_loop(0, P_DEV, place, grad_acc)
        terms = jnp.stack([window_re * update_re + window_im * update_im, window_re * update_im - window_im * update_re], axis=1).astype(jnp.bfloat16)
        partial_sum = jnp.dot(mixing.T, terms.reshape(P_DEV, -1).astype(jnp.float32), precision=lax.Precision.HIGHEST)
        partial_sum = lax.optimization_barrier(partial_sum.astype(jnp.bfloat16)).astype(jnp.float32).reshape(2 * K, 2, W, W)
        mode_acc = mode_acc.at[row_id].add(partial_sum[:K])
        mode_acc = mode_acc.at[next_row].add(partial_sum[K:])
        return ((grad_acc, mode_acc), None)
    (grad_acc, mode_acc), _ = lax.scan(tile_step, (grad_init, modes_init), jnp.arange(REGIONS * TILE_COLS, dtype=jnp.int32))
    return (grad_acc[:, half_size:-half_size, half_size:-half_size], mode_acc)
```

```python
import functools
import math

import jax
import jax.numpy as jnp
import numpy as np
from jax import lax
from jax.experimental import pallas as pl
from jax.experimental.pallas import tpu as pltpu
from jax.sharding import PartitionSpec as P

FLOOR = 0.25
PAD = 128
SLOT_ROWS = 8
F32 = jnp.float32
BF16 = jnp.bfloat16
MESH = pl.DeviceIdType.MESH


def dft_blocks(length):
    index = np.arange(length)
    angles = (index[:, None] * index[None, :] % length).astype(np.float32) * np.float32(2.0 * math.pi / length)
    scaling = np.float32(1.0 / math.sqrt(length))
    re = (np.cos(angles) * scaling).astype(jnp.bfloat16)
    im = (-np.sin(angles) * scaling).astype(jnp.bfloat16)
    block = np.block([[re, -im], [im, re]])
    return block, np.ascontiguousarray(block.T)


def dot(a, b):
    return jnp.dot(a, b, preferred_element_type=F32)


def iota(shape, dim):
    return lax.broadcasted_iota(jnp.int32, shape, dim)


def where_bf16(mask):
    return jnp.where(mask, 1.0, 0.0).astype(BF16)


def kernel(
    dims,
    place_ref, count_ref, object_ref, modes_ref, mix_ref, inten_hbm, m_hbm, mt_hbm,
    grad_ref, mode_ref,
    ext, nxt, mixes, stack, kron, kron_t, share, probes, windows, inten, m_ref, mt_ref,
    terms, got_terms, acc, out_cols, got_cols, out_rows, got_rows, sums, out_sums, got_sums,
    local_sem, pair_send, pair_recv, mix_send, mix_recv, probe_send, probe_recv, term_send, term_recv,
):
    rows, cols, slots, num_modes, strip = dims
    size = cols * strip
    half = size // 2
    full = 2 * size
    width = 2 * num_modes * strip
    r, c = lax.axis_index("row"), lax.axis_index("col")
    north, south = lax.rem(r + rows - 1, rows), lax.rem(r + 1, rows)
    west, east = lax.rem(c + cols - 1, cols), lax.rem(c + 1, cols)

    def remote(src, dst, index, device):
        return pltpu.make_async_remote_copy(
            src_ref=src, dst_ref=dst, send_sem=pair_send.at[index], recv_sem=pair_recv.at[index],
            device_id=device, device_id_type=MESH,
        )

    def everyone(body):
        def step(k, carry):
            body(lax.rem(c + k, cols))
            return carry

        lax.fori_loop(1, cols, step, 0)

    loads = [
        pltpu.make_async_copy(src, dst, local_sem.at[i])
        for i, (src, dst) in enumerate([(inten_hbm, inten), (m_hbm, m_ref), (mt_hbm, mt_ref)])
    ]
    for load in loads:
        load.start()

    barrier = pltpu.get_barrier_semaphore()
    everyone(lambda peer: pl.semaphore_signal(barrier, inc=1, device_id={"col": peer}, device_id_type=MESH))
    for peer in (north, south):
        pl.semaphore_signal(barrier, inc=1, device_id={"row": peer}, device_id_type=MESH)
    inner = pl.ds(half, size)
    low, high = pl.ds(half, half), pl.ds(size, half)
    first, last = pl.ds(0, half), pl.ds(size + half, half)
    ext[:, inner, inner] = object_ref[...].astype(BF16)
    mixes[c] = mix_ref[...]
    pl.semaphore_wait(barrier, cols + 1)

    send_modes = remote(modes_ref, nxt, 0, {"row": north})
    send_modes.start()

    def mix_copy(peer):
        return pltpu.make_async_remote_copy(
            src_ref=mix_ref, dst_ref=mixes.at[c], send_sem=mix_send, recv_sem=mix_recv,
            device_id={"col": peer}, device_id_type=MESH,
        )

    everyone(lambda peer: mix_copy(peer).start())
    to_north = remote(ext.at[:, low, inner], ext.at[:, last, inner], 1, {"row": north})
    to_south = remote(ext.at[:, high, inner], ext.at[:, first, inner], 2, {"row": south})
    to_west = remote(ext.at[:, inner, low], ext.at[:, inner, last], 3, {"col": west})
    to_east = remote(ext.at[:, inner, high], ext.at[:, inner, first], 4, {"col": east})
    for copy in (to_north, to_south, to_west, to_east):
        copy.start()

    others = pl.ds(0, cols - 1)
    pltpu.make_async_copy(mixes.at[others], mixes.at[others], mix_recv).wait()
    mixed = mixes[...].reshape(cols * SLOT_ROWS, PAD)
    coarse = mixed.astype(BF16)
    fine = (mixed - coarse.astype(F32)).astype(BF16)
    repeat = where_bf16(iota((PAD, width), 0) == lax.div(iota((PAD, width), 1), strip))
    diagonal = iota((strip, width), 0) == lax.rem(iota((strip, width), 1), strip)
    for i, part in enumerate((coarse, fine)):
        wide = dot(part, repeat).reshape(cols, SLOT_ROWS, width)
        for p in range(slots):
            block = jnp.where(diagonal[None], wide[:, p : p + 1, :], 0.0)
            kron[i, p] = block.reshape(size, width).astype(BF16)

    send_modes.wait_recv()
    for plane in range(2):
        lanes = pl.ds(plane * size, size)
        stack[: width // 2, lanes] = modes_ref[:, plane].reshape(width // 2, size)
        stack[width // 2 :, lanes] = nxt[:, plane].reshape(width // 2, size)

    def probe_copy(p, peer):
        return pltpu.make_async_remote_copy(
            src_ref=share.at[p, peer], dst_ref=probes.at[p, c], send_sem=probe_send.at[p], recv_sem=probe_recv.at[p],
            device_id={"col": peer}, device_id_type=MESH,
        )

    def mix_slot(p):
        both = dot(kron[0, p], stack[...]) + dot(kron[1, p], stack[...])
        for plane in range(2):
            part = both[:, plane * size : (plane + 1) * size].astype(BF16)
            share[p, :, plane] = part.reshape(cols, strip, size)
        probes[p, c] = share[p, c]
        everyone(lambda peer: probe_copy(p, peer).start())

    mix_slot(0)
    to_south.wait_recv()
    north_west = remote(ext.at[:, first, low], ext.at[:, first, last], 5, {"col": west})
    north_east = remote(ext.at[:, first, high], ext.at[:, first, first], 6, {"col": east})
    north_west.start()
    north_east.start()
    to_north.wait_recv()
    south_west = remote(ext.at[:, last, low], ext.at[:, last, last], 7, {"col": west})
    south_east = remote(ext.at[:, last, high], ext.at[:, last, first], 8, {"col": east})
    south_west.start()
    south_east.start()
    for p in range(1, slots):
        mix_slot(p)

    repeat_t = where_bf16(iota((width, PAD), 1) == lax.div(iota((width, PAD), 0), strip))
    diagonal_t = lax.rem(iota((width, size), 0), strip) == lax.rem(iota((width, size), 1), strip)
    for i, part in enumerate((coarse, fine)):
        wide_t = lax.dot_general(repeat_t, part, (((1,), (1,)), ((), ())), preferred_element_type=F32).astype(BF16)
        for p in range(slots):
            sel_shape = (cols * SLOT_ROWS, size)
            select = where_bf16(iota(sel_shape, 0) == lax.div(iota(sel_shape, 1), strip) * SLOT_ROWS + p)
            kron_t[i, p] = jnp.where(diagonal_t, dot(wide_t, select), 0.0).astype(BF16)
    acc[...] = jnp.zeros_like(acc)

    for copy in (to_west, to_east, north_west, north_east, south_west, south_east):
        copy.wait_recv()
    for copy in (to_north, to_south, to_west, to_east, north_west, north_east, south_west, south_east):
        copy.wait_send()
    for edge, box in (
        (r == 0, (slice(None), first, slice(None))),
        (r == rows - 1, (slice(None), last, slice(None))),
        (c == 0, (slice(None), pl.ds(0, full), first)),
        (c == cols - 1, (slice(None), pl.ds(0, full), last)),
    ):

        @pl.when(edge)
        def _(box=box):
            ext[box] = jnp.zeros_like(ext[box])

    def cut(p, carry):
        pick_rows = where_bf16(iota((size, full), 1) == iota((size, full), 0) + place_ref[p, 0])
        pick_cols = where_bf16(iota((full, size), 0) == iota((full, size), 1) + place_ref[p, 1])
        for plane in range(2):
            narrow = dot(ext[plane], pick_cols).astype(BF16)
            windows[p, plane] = dot(pick_rows, narrow).astype(BF16)
        return carry

    lax.fori_loop(0, slots, cut, 0)
    for load in loads:
        load.wait()

    def term_copy(p, peer):
        return pltpu.make_async_remote_copy(
            src_ref=terms.at[p, peer], dst_ref=got_terms.at[p, c], send_sem=term_send.at[p], recv_sem=term_recv.at[p],
            device_id={"col": peer}, device_id_type=MESH,
        )

    def position(p, carry):
        pltpu.make_async_copy(probes.at[p, others], probes.at[p, others], probe_recv.at[p]).wait()
        pr_re = probes[p, :, 0].reshape(size, size).astype(F32)
        pr_im = probes[p, :, 1].reshape(size, size).astype(F32)
        w_re = windows[p, 0].astype(F32)
        w_im = windows[p, 1].astype(F32)
        e_re = (pr_re * w_re - pr_im * w_im).astype(BF16)
        e_im = (pr_re * w_im + pr_im * w_re).astype(BF16)
        left = dot(m_ref[...], jnp.concatenate([e_re, e_im], axis=0)).astype(BF16)
        far = dot(jnp.concatenate([left[:size], left[size:]], axis=1), mt_ref[...])
        f_re, f_im = far[:, :size], far[:, size:]
        energy = jnp.maximum(f_re * f_re + f_im * f_im, FLOOR * FLOOR)
        live = jnp.where(p < count_ref[0, 0], 1.0, 0.0).astype(F32)
        factor = (jnp.sqrt(inten[p].astype(F32)) * lax.rsqrt(energy) - 1.0) * live
        c_re = (f_re * factor).astype(BF16)
        c_im = (f_im * factor).astype(BF16)
        back = dot(mt_ref[...], jnp.concatenate([c_re, c_im], axis=0)).astype(BF16)
        update = dot(jnp.concatenate([back[:size], back[size:]], axis=1), m_ref[...])
        u_re, u_im = update[:, :size], update[:, size:]
        terms[p, :, 0] = (w_re * u_re + w_im * u_im).astype(BF16).reshape(cols, strip, size)
        terms[p, :, 1] = (w_re * u_im - w_im * u_re).astype(BF16).reshape(cols, strip, size)
        got_terms[p, c] = terms[p, c]
        everyone(lambda peer: term_copy(p, peer).start())
        put_rows = where_bf16(iota((full, size), 0) == iota((full, size), 1) + place_ref[p, 0])
        put_cols = where_bf16(iota((size, full), 1) == iota((size, full), 0) + place_ref[p, 1])
        for plane, value in enumerate((pr_re * u_re + pr_im * u_im, pr_re * u_im - pr_im * u_re)):
            acc[plane] += dot(put_rows, dot(value.astype(BF16), put_cols).astype(BF16))
        return carry

    lax.fori_loop(0, slots, position, 0)

    out_cols[0] = acc[:, :, first].astype(BF16)
    out_cols[1] = acc[:, :, last].astype(BF16)
    cols_west = remote(out_cols.at[0], got_cols.at[1], 9, {"col": west})
    cols_east = remote(out_cols.at[1], got_cols.at[0], 10, {"col": east})
    cols_west.start()
    cols_east.start()

    def gather(p):
        pltpu.make_async_copy(got_terms.at[p, others], got_terms.at[p, others], term_recv.at[p]).wait()
        both = jnp.concatenate([got_terms[p, :, plane].reshape(size, size) for plane in range(2)], axis=1)
        return dot(kron_t[0, p], both) + dot(kron_t[1, p], both)

    sums[...] = gather(0)
    for p in range(1, slots - 1):
        sums[...] += gather(p)

    cols_east.wait_recv()
    acc[:, :, low] += jnp.where(c == 0, 0.0, got_cols[0].astype(F32))
    cols_west.wait_recv()
    acc[:, :, high] += jnp.where(c == cols - 1, 0.0, got_cols[1].astype(F32))
    out_rows[0] = acc[:, first, inner].astype(BF16)
    out_rows[1] = acc[:, last, inner].astype(BF16)
    rows_north = remote(out_rows.at[0], got_rows.at[1], 11, {"row": north})
    rows_south = remote(out_rows.at[1], got_rows.at[0], 12, {"row": south})
    rows_north.start()
    rows_south.start()

    sums[...] += gather(slots - 1)
    for plane in range(2):
        part = sums[width // 2 :, pl.ds(plane * size, size)].astype(BF16)
        out_sums[:, plane] = part.reshape(num_modes, strip, size)
    send_sums = remote(out_sums, got_sums, 13, {"row": south})
    send_sums.start()

    rows_south.wait_recv()
    grad_ref[:, pl.ds(0, half), :] = acc[:, low, inner] + jnp.where(r == 0, 0.0, got_rows[0].astype(F32))
    rows_north.wait_recv()
    grad_ref[:, pl.ds(half, half), :] = acc[:, high, inner] + jnp.where(r == rows - 1, 0.0, got_rows[1].astype(F32))
    send_sums.wait_recv()
    for plane in range(2):
        own = sums[: width // 2, pl.ds(plane * size, size)].reshape(num_modes, strip, size)
        mode_ref[:, plane] = own + got_sums[:, plane].astype(F32)

    for copy in (send_modes, cols_west, cols_east, rows_north, rows_south, send_sums):
        copy.wait_send()
    pltpu.make_async_copy(mixes.at[others], mixes.at[others], mix_send).wait()
    for p in range(slots):
        pltpu.make_async_copy(share.at[p, others], share.at[p, others], probe_send.at[p]).wait()
        pltpu.make_async_copy(terms.at[p, others], terms.at[p, others], term_send.at[p]).wait()


def local(object_field, modes, coeffs, offsets, region, counts, intensity):
    size = modes.shape[-1]
    half = size // 2
    full = 2 * size
    num_modes = modes.shape[1]
    slots = coeffs.shape[2]
    strip = modes.shape[3]
    rows, cols = lax.axis_size("row"), lax.axis_size("col")
    row_index = lax.axis_index("row")
    weights = coeffs[0, 0]
    regions = region[0, 0]
    own_mask = (regions == row_index).astype(F32)
    next_mask = (regions == row_index + 1).astype(F32)
    mixing = jnp.concatenate([weights * own_mask[:, None], weights * next_mask[:, None]], axis=1)
    mixing = jnp.pad(mixing, ((0, SLOT_ROWS - slots), (0, PAD - 2 * num_modes)))
    place = offsets[0, 0] + half
    block, block_t = dft_blocks(size)
    width = 2 * num_modes * strip
    vmem = pl.BlockSpec(memory_space=pltpu.VMEM)
    smem = pl.BlockSpec(memory_space=pltpu.SMEM)
    hbm = pl.BlockSpec(memory_space=pl.ANY)
    pieces = (slots, cols, 2, strip, size)
    dma = pltpu.SemaphoreType.DMA
    object_grad, mode_grad = pl.pallas_call(
        functools.partial(kernel, (rows, cols, slots, num_modes, strip)),
        out_shape=(
            jax.ShapeDtypeStruct((2, size, size), F32),
            jax.ShapeDtypeStruct((num_modes, 2, strip, size), F32),
        ),
        in_specs=[smem, smem, vmem, vmem, vmem, hbm, hbm, hbm],
        out_specs=(vmem, vmem),
        scratch_shapes=[
            pltpu.VMEM((2, full, full), BF16),
            pltpu.VMEM((num_modes, 2, strip, size), BF16),
            pltpu.VMEM((cols, SLOT_ROWS, PAD), F32),
            pltpu.VMEM((width, full), BF16),
            pltpu.VMEM((2, slots, size, width), BF16),
            pltpu.VMEM((2, slots, width, size), BF16),
            pltpu.VMEM(pieces, BF16),
            pltpu.VMEM(pieces, BF16),
            pltpu.VMEM((slots, 2, size, size), BF16),
            pltpu.VMEM((slots, size, size), BF16),
            pltpu.VMEM((full, full), BF16),
            pltpu.VMEM((full, full), BF16),
            pltpu.VMEM(pieces, BF16),
            pltpu.VMEM(pieces, BF16),
            pltpu.VMEM((2, full, full), F32),
            pltpu.VMEM((2, 2, full, half), BF16),
            pltpu.VMEM((2, 2, full, half), BF16),
            pltpu.VMEM((2, 2, half, size), BF16),
            pltpu.VMEM((2, 2, half, size), BF16),
            pltpu.VMEM((width, full), F32),
            pltpu.VMEM((num_modes, 2, strip, size), BF16),
            pltpu.VMEM((num_modes, 2, strip, size), BF16),
            dma((3,)),
            dma((14,)),
            dma((14,)),
            dma,
            dma,
            dma((slots,)),
            dma((slots,)),
            dma((slots,)),
            dma((slots,)),
        ],
        compiler_params=pltpu.CompilerParams(
            collective_id=0, has_side_effects=True, vmem_limit_bytes=56 << 20
        ),
        name="ptychography",
    )(place, counts, object_field, modes[0], mixing, intensity[0, 0], jnp.asarray(block), jnp.asarray(block_t))
    return object_grad, mode_grad[None]


def solution(mesh):
    in_specs = (
        P(None, "row", "col"),
        P("row", None, None, "col", None),
        P("row", "col", None, None),
        P("row", "col", None, None),
        P("row", "col", None),
        P("row", "col"),
        P("row", "col", None, None, None),
    )
    out_specs = (P(None, "row", "col"), P("row", None, None, "col", None))
    return jax.shard_map(local, mesh=mesh, in_specs=in_specs, out_specs=out_specs, check_vma=False)
```

```python
import functools
import math

import jax
import jax.numpy as jnp
import numpy as np
from jax import lax
from jax.experimental import pallas as pl
from jax.experimental.pallas import tpu as pltpu
from jax.sharding import PartitionSpec as P

FLOOR = 0.25
PAD = 128
SLOT_ROWS = 8
F32 = jnp.float32
BF16 = jnp.bfloat16
MESH = pl.DeviceIdType.MESH


def dft_blocks(length):
    index = np.arange(length)
    angles = (index[:, None] * index[None, :] % length).astype(np.float32) * np.float32(2.0 * math.pi / length)
    scaling = np.float32(1.0 / math.sqrt(length))
    re = (np.cos(angles) * scaling).astype(jnp.bfloat16)
    im = (-np.sin(angles) * scaling).astype(jnp.bfloat16)
    block = np.block([[re, -im], [im, re]])
    return block, np.ascontiguousarray(block.T)


def dot(a, b):
    return jnp.dot(a, b, preferred_element_type=F32)


def iota(shape, dim):
    return lax.broadcasted_iota(jnp.int32, shape, dim)


def where_bf16(mask):
    return jnp.where(mask, 1.0, 0.0).astype(BF16)


def kernel(
    dims,
    object_hbm, modes_hbm, coeffs_hbm, offsets_hbm, region_hbm, counts_hbm, inten_hbm, m_hbm, mt_hbm,
    grad_ref, mode_ref,
    object_ref, modes_ref, coeffs_ref, offsets_ref, region_ref, counts_ref, inten, m_ref, mt_ref,
    ext, nxt, mixes, stack, kron, kron_t, share, probes, windows,
    terms, got_terms, acc, out_cols, got_cols, out_rows, got_rows, sums, out_sums, got_sums,
    local_sem, pair_send, pair_recv, mix_send, mix_recv, probe_send, probe_recv, term_send, term_recv,
):
    rows, cols, slots, num_modes, strip = dims
    size = cols * strip
    half = size // 2
    full = 2 * size
    split = num_modes * strip
    width = 2 * split
    r, c = lax.axis_index("row"), lax.axis_index("col")
    north, south = lax.rem(r + rows - 1, rows), lax.rem(r + 1, rows)
    west, east = lax.rem(c + cols - 1, cols), lax.rem(c + 1, cols)
    inner = pl.ds(half, size)
    low, high = pl.ds(half, half), pl.ds(size, half)
    first, last = pl.ds(0, half), pl.ds(size + half, half)
    others = pl.ds(0, cols - 1)

    def remote(src, dst, index, device):
        return pltpu.make_async_remote_copy(
            src_ref=src, dst_ref=dst, send_sem=pair_send.at[index], recv_sem=pair_recv.at[index],
            device_id=device, device_id_type=MESH,
        )

    def scatter(src, dst, send_sem, recv_sem, peer):
        return pltpu.make_async_remote_copy(
            src_ref=src, dst_ref=dst, send_sem=send_sem, recv_sem=recv_sem,
            device_id={"col": peer}, device_id_type=MESH,
        )

    def everyone(body):
        def step(k, carry):
            body(lax.rem(c + k, cols))
            return carry

        lax.fori_loop(1, cols, step, 0)

    def arrived(buffer, sem):
        pltpu.make_async_copy(buffer, buffer, sem).wait()

    barrier = pltpu.get_barrier_semaphore()
    everyone(lambda peer: pl.semaphore_signal(barrier, inc=1, device_id={"col": peer}, device_id_type=MESH))
    for peer in (north, south):
        pl.semaphore_signal(barrier, inc=1, device_id={"row": peer}, device_id_type=MESH)
    pairs = [
        (coeffs_hbm, coeffs_ref), (region_hbm, region_ref), (modes_hbm, modes_ref), (object_hbm, object_ref),
        (offsets_hbm, offsets_ref), (counts_hbm, counts_ref), (inten_hbm, inten), (m_hbm, m_ref), (mt_hbm, mt_ref),
    ]
    loads = [pltpu.make_async_copy(src, dst, local_sem.at[i]) for i, (src, dst) in enumerate(pairs)]
    for load in loads:
        load.start()
    for load in loads[:2]:
        load.wait()
    mixes[c] = jnp.zeros((SLOT_ROWS, PAD), F32)
    for p in range(slots):
        weights = coeffs_ref[0, 0, p : p + 1, :]
        area = region_ref[0, :, p : p + 1]
        mixes[c, p : p + 1, :num_modes] = jnp.where(area == r, weights, 0.0)
        mixes[c, p : p + 1, num_modes : 2 * num_modes] = jnp.where(area == r + 1, weights, 0.0)
    for load in loads[2:4]:
        load.wait()
    ext[:, inner, inner] = object_ref[...].astype(BF16)
    pl.semaphore_wait(barrier, cols + 1)

    everyone(lambda peer: scatter(mixes.at[c], mixes.at[c], mix_send, mix_recv, peer).start())
    send_modes = remote(modes_ref, nxt, 0, {"row": north})
    send_modes.start()
    to_north = remote(ext.at[:, low, inner], ext.at[:, last, inner], 1, {"row": north})
    to_south = remote(ext.at[:, high, inner], ext.at[:, first, inner], 2, {"row": south})
    to_west = remote(ext.at[:, inner, low], ext.at[:, inner, last], 3, {"col": west})
    to_east = remote(ext.at[:, inner, high], ext.at[:, inner, first], 4, {"col": east})
    for copy in (to_north, to_south, to_west, to_east):
        copy.start()

    def stack_modes(modes, start):
        for plane in range(2):
            stack[start : start + split, pl.ds(plane * size, size)] = modes[:, plane].reshape(split, size)

    stack_modes(modes_ref.at[0], 0)
    stack[split:] = jnp.zeros((split, full), BF16)

    arrived(mixes.at[others], mix_recv)
    mixed = mixes[...].reshape(cols * SLOT_ROWS, PAD)
    coarse = mixed.astype(BF16)
    fine = (mixed - coarse.astype(F32)).astype(BF16)
    repeat = where_bf16(iota((PAD, width), 0) == lax.div(iota((PAD, width), 1), strip))
    diagonal = iota((strip, width), 0) == lax.rem(iota((strip, width), 1), strip)
    for i, part in enumerate((coarse, fine)):
        wide = dot(part, repeat).reshape(cols, SLOT_ROWS, width)
        for p in range(slots):
            block = jnp.where(diagonal[None], wide[:, p : p + 1, :], 0.0)
            kron[i, p] = block.reshape(size, width).astype(BF16)

    def mix_slot(p):
        both = dot(kron[0, p], stack[...]) + dot(kron[1, p], stack[...])
        for plane in range(2):
            part = both[:, plane * size : (plane + 1) * size].astype(BF16)
            share[p, :, plane] = part.reshape(cols, strip, size)
        everyone(
            lambda peer: scatter(share.at[p, peer], probes.at[p, c], probe_send.at[p], probe_recv.at[p], peer).start()
        )
        probes[p, c] = share[p, c]

    mix_slot(0)
    send_modes.wait_recv()
    stack_modes(nxt.at[0], split)
    mix_slot(1)
    to_south.wait_recv()
    north_west = remote(ext.at[:, first, low], ext.at[:, first, last], 5, {"col": west})
    north_east = remote(ext.at[:, first, high], ext.at[:, first, first], 6, {"col": east})
    north_west.start()
    north_east.start()
    to_north.wait_recv()
    south_west = remote(ext.at[:, last, low], ext.at[:, last, last], 7, {"col": west})
    south_east = remote(ext.at[:, last, high], ext.at[:, last, first], 8, {"col": east})
    south_west.start()
    south_east.start()
    for p in range(2, slots):
        mix_slot(p)

    repeat_t = where_bf16(iota((width, PAD), 1) == lax.div(iota((width, PAD), 0), strip))
    diagonal_t = lax.rem(iota((width, size), 0), strip) == lax.rem(iota((width, size), 1), strip)
    for i, part in enumerate((coarse, fine)):
        wide_t = lax.dot_general(repeat_t, part, (((1,), (1,)), ((), ())), preferred_element_type=F32).astype(BF16)
        for p in range(slots):
            sel_shape = (cols * SLOT_ROWS, size)
            select = where_bf16(iota(sel_shape, 0) == lax.div(iota(sel_shape, 1), strip) * SLOT_ROWS + p)
            kron_t[i, p] = jnp.where(diagonal_t, dot(wide_t, select), 0.0).astype(BF16)
    acc[...] = jnp.zeros_like(acc)
    for load in loads[4:]:
        load.wait()

    for copy in (to_west, to_east, north_west, north_east, south_west, south_east):
        copy.wait_recv()
    for copy in (to_north, to_south, to_west, to_east, north_west, north_east, south_west, south_east):
        copy.wait_send()
    for edge, box in (
        (r == 0, (slice(None), first, slice(None))),
        (r == rows - 1, (slice(None), last, slice(None))),
        (c == 0, (slice(None), pl.ds(0, full), first)),
        (c == cols - 1, (slice(None), pl.ds(0, full), last)),
    ):

        @pl.when(edge)
        def _(box=box):
            ext[box] = jnp.zeros_like(ext[box])

    def corner(p, axis):
        return offsets_ref[0, 0, axis : axis + 1, p : p + 1] + half

    for p in range(slots):
        pick_rows = where_bf16(iota((size, full), 1) == iota((size, full), 0) + corner(p, 0))
        pick_cols = where_bf16(iota((full, size), 0) == iota((full, size), 1) + corner(p, 1))
        for plane in range(2):
            narrow = dot(ext[plane], pick_cols).astype(BF16)
            windows[p, plane] = dot(pick_rows, narrow).astype(BF16)

    def send_terms(p):
        everyone(
            lambda peer: scatter(terms.at[p, peer], got_terms.at[p, c], term_send.at[p], term_recv.at[p], peer).start()
        )
        got_terms[p, c] = terms[p, c]

    def position(p):
        arrived(probes.at[p, others], probe_recv.at[p])
        pr_re = probes[p, :, 0].reshape(size, size).astype(F32)
        pr_im = probes[p, :, 1].reshape(size, size).astype(F32)
        w_re = windows[p, 0].astype(F32)
        w_im = windows[p, 1].astype(F32)
        e_re = (pr_re * w_re - pr_im * w_im).astype(BF16)
        e_im = (pr_re * w_im + pr_im * w_re).astype(BF16)
        left = dot(m_ref[...], jnp.concatenate([e_re, e_im], axis=0)).astype(BF16)
        far = dot(jnp.concatenate([left[:size], left[size:]], axis=1), mt_ref[...])
        f_re, f_im = far[:, :size], far[:, size:]
        energy = jnp.maximum(f_re * f_re + f_im * f_im, FLOOR * FLOOR)
        live = jnp.where(counts_ref[...] > p, 1.0, 0.0)
        factor = (jnp.sqrt(inten[0, 0, p].astype(F32)) * lax.rsqrt(energy) - 1.0) * live
        c_re = (f_re * factor).astype(BF16)
        c_im = (f_im * factor).astype(BF16)
        back = dot(mt_ref[...], jnp.concatenate([c_re, c_im], axis=0)).astype(BF16)
        update = dot(jnp.concatenate([back[:size], back[size:]], axis=1), m_ref[...])
        u_re, u_im = update[:, :size], update[:, size:]
        terms[p, :, 0] = (w_re * u_re + w_im * u_im).astype(BF16).reshape(cols, strip, size)
        terms[p, :, 1] = (w_re * u_im - w_im * u_re).astype(BF16).reshape(cols, strip, size)
        if p < slots - 1:
            send_terms(p)
        put_rows = where_bf16(iota((full, size), 0) == iota((full, size), 1) + corner(p, 0))
        put_cols = where_bf16(iota((size, full), 1) == iota((size, full), 0) + corner(p, 1))
        for plane, value in enumerate((pr_re * u_re + pr_im * u_im, pr_re * u_im - pr_im * u_re)):
            acc[plane] += dot(put_rows, dot(value.astype(BF16), put_cols).astype(BF16))

    for p in range(slots):
        position(p)

    out_cols[0] = acc[:, :, first].astype(BF16)
    out_cols[1] = acc[:, :, last].astype(BF16)
    cols_west = remote(out_cols.at[0], got_cols.at[1], 9, {"col": west})
    cols_east = remote(out_cols.at[1], got_cols.at[0], 10, {"col": east})
    cols_west.start()
    cols_east.start()
    send_terms(slots - 1)

    def gather(p, half_of):
        both = jnp.concatenate([got_terms[p, :, plane].reshape(size, size) for plane in range(2)], axis=1)
        spot = pl.ds(half_of * split, split)
        value = dot(kron_t[0, p, spot], both) + dot(kron_t[1, p, spot], both)
        if p == 0:
            sums[spot] = value
        else:
            sums[spot] += value

    for p in range(slots - 2):
        arrived(got_terms.at[p, others], term_recv.at[p])
        gather(p, 1)

    cols_east.wait_recv()
    acc[:, :, low] += jnp.where(c == 0, 0.0, got_cols[0].astype(F32))
    cols_west.wait_recv()
    acc[:, :, high] += jnp.where(c == cols - 1, 0.0, got_cols[1].astype(F32))
    out_rows[0] = acc[:, first, inner].astype(BF16)
    out_rows[1] = acc[:, last, inner].astype(BF16)
    rows_north = remote(out_rows.at[0], got_rows.at[1], 11, {"row": north})
    rows_south = remote(out_rows.at[1], got_rows.at[0], 12, {"row": south})
    rows_north.start()
    rows_south.start()

    for p in range(slots - 2, slots):
        arrived(got_terms.at[p, others], term_recv.at[p])
        gather(p, 1)
    for plane in range(2):
        part = sums[split:, pl.ds(plane * size, size)].astype(BF16)
        out_sums[:, plane] = part.reshape(num_modes, strip, size)
    send_sums = remote(out_sums, got_sums, 13, {"row": south})
    send_sums.start()
    for p in range(slots):
        gather(p, 0)

    rows_south.wait_recv()
    grad_ref[:, pl.ds(0, half), :] = acc[:, low, inner] + jnp.where(r == 0, 0.0, got_rows[0].astype(F32))
    rows_north.wait_recv()
    grad_ref[:, pl.ds(half, half), :] = acc[:, high, inner] + jnp.where(r == rows - 1, 0.0, got_rows[1].astype(F32))
    send_sums.wait_recv()
    for plane in range(2):
        own = sums[:split, pl.ds(plane * size, size)].reshape(num_modes, strip, size)
        mode_ref[0, :, plane] = own + got_sums[:, plane].astype(F32)

    for copy in (send_modes, cols_west, cols_east, rows_north, rows_south, send_sums):
        copy.wait_send()
    arrived(mixes.at[others], mix_send)
    for p in range(slots):
        arrived(share.at[p, others], probe_send.at[p])
        arrived(terms.at[p, others], term_send.at[p])


def local(object_field, modes, coeffs, offsets, region, counts, intensity):
    size = modes.shape[-1]
    half = size // 2
    full = 2 * size
    num_modes = modes.shape[1]
    slots = coeffs.shape[2]
    strip = modes.shape[3]
    rows, cols = lax.axis_size("row"), lax.axis_size("col")
    block, block_t = dft_blocks(size)
    width = 2 * num_modes * strip
    vmem = pl.BlockSpec(memory_space=pltpu.VMEM)
    hbm = pl.BlockSpec(memory_space=pl.ANY)
    pieces = (slots, cols, 2, strip, size)
    dma = pltpu.SemaphoreType.DMA
    args = (
        object_field, modes, coeffs, jnp.swapaxes(offsets, 2, 3), region, counts, intensity, jnp.asarray(block), jnp.asarray(block_t),
    )
    return pl.pallas_call(
        functools.partial(kernel, (rows, cols, slots, num_modes, strip)),
        out_shape=(
            jax.ShapeDtypeStruct((2, size, size), F32),
            jax.ShapeDtypeStruct((1, num_modes, 2, strip, size), F32),
        ),
        in_specs=[hbm] * len(args),
        out_specs=(vmem, vmem),
        scratch_shapes=[pltpu.VMEM(x.shape, x.dtype) for x in args]
        + [
            pltpu.VMEM((2, full, full), BF16),
            pltpu.VMEM(modes.shape, BF16),
            pltpu.VMEM((cols, SLOT_ROWS, PAD), F32),
            pltpu.VMEM((width, full), BF16),
            pltpu.VMEM((2, slots, size, width), BF16),
            pltpu.VMEM((2, slots, width, size), BF16),
            pltpu.VMEM(pieces, BF16),
            pltpu.VMEM(pieces, BF16),
            pltpu.VMEM((slots, 2, size, size), BF16),
            pltpu.VMEM(pieces, BF16),
            pltpu.VMEM(pieces, BF16),
            pltpu.VMEM((2, full, full), F32),
            pltpu.VMEM((2, 2, full, half), BF16),
            pltpu.VMEM((2, 2, full, half), BF16),
            pltpu.VMEM((2, 2, half, size), BF16),
            pltpu.VMEM((2, 2, half, size), BF16),
            pltpu.VMEM((width, full), F32),
            pltpu.VMEM((num_modes, 2, strip, size), BF16),
            pltpu.VMEM((num_modes, 2, strip, size), BF16),
            dma((len(args),)),
            dma((14,)),
            dma((14,)),
            dma,
            dma,
            dma((slots,)),
            dma((slots,)),
            dma((slots,)),
            dma((slots,)),
        ],
        compiler_params=pltpu.CompilerParams(
            collective_id=0, has_side_effects=True, vmem_limit_bytes=56 << 20
        ),
        name="ptychography",
    )(*args)


def solution(mesh):
    in_specs = (
        P(None, "row", "col"),
        P("row", None, None, "col", None),
        P("row", "col", None, None),
        P("row", "col", None, None),
        P("row", "col", None),
        P("row", "col"),
        P("row", "col", None, None, None),
    )
    out_specs = (P(None, "row", "col"), P("row", None, None, "col", None))
    return jax.shard_map(local, mesh=mesh, in_specs=in_specs, out_specs=out_specs, check_vma=False)
```

```python
import functools
import math

import jax
import jax.numpy as jnp
import numpy as np
from jax import lax
from jax.experimental import pallas as pl
from jax.experimental.pallas import tpu as pltpu
from jax.sharding import PartitionSpec as P

FLOOR = 0.25
PAD = 128
SLOT_ROWS = 8
F32 = jnp.float32
BF16 = jnp.bfloat16
MESH = pl.DeviceIdType.MESH


def dft_blocks(length):
    index = np.arange(length)
    angles = (index[:, None] * index[None, :] % length).astype(np.float32) * np.float32(2.0 * math.pi / length)
    scaling = np.float32(1.0 / math.sqrt(length))
    re = (np.cos(angles) * scaling).astype(jnp.bfloat16)
    im = (-np.sin(angles) * scaling).astype(jnp.bfloat16)
    block = np.block([[re, -im], [im, re]])
    return block, np.ascontiguousarray(block.T)


def dot(a, b):
    return jnp.dot(a, b, preferred_element_type=F32)


def iota(shape, dim):
    return lax.broadcasted_iota(jnp.int32, shape, dim)


def where_bf16(mask):
    return jnp.where(mask, 1.0, 0.0).astype(BF16)


def kernel(
    dims,
    object_hbm, modes_hbm, coeffs_hbm, offsets_hbm, region_hbm, counts_hbm, inten_hbm, m_hbm, mt_hbm,
    grad_ref, mode_ref,
    object_ref, modes_ref, coeffs_ref, offsets_ref, region_ref, counts_ref, inten, m_ref, mt_ref,
    ext, nxt, mixes, stack, kron, kron_t, share, probes, windows,
    help_own, help_nxt, help_stack, help_share, carried, carried_out,
    terms, got_terms, acc, out_cols, got_cols, out_rows, got_rows, sums, out_sums, got_sums,
    local_sem, pair_send, pair_recv, mix_send, mix_recv, probe_send, probe_recv, term_send, term_recv,
):
    rows, cols, slots, num_modes, strip = dims
    size = cols * strip
    half = size // 2
    full = 2 * size
    split = num_modes * strip
    width = 2 * split
    r, c = lax.axis_index("row"), lax.axis_index("col")
    north, south = lax.rem(r + rows - 1, rows), lax.rem(r + 1, rows)
    west, east = lax.rem(c + cols - 1, cols), lax.rem(c + 1, cols)
    inner = pl.ds(half, size)
    low, high = pl.ds(half, half), pl.ds(size, half)
    first, last = pl.ds(0, half), pl.ds(size + half, half)
    others = pl.ds(0, cols - 1)
    side = cols // 4
    block = cols // 2
    plane, spot = lax.div(c, side), lax.rem(c, side)
    group = lax.div(c, block)
    outer = (plane == 0) | (plane == 3)
    helper = (plane == 1) | (plane == 2)
    across = lax.rem(c + block, cols)
    even = lax.rem(r, 2) == 0
    has_west, has_east = c > 0, c < cols - 1
    turn_west = (spot == 0) & has_west
    turn_east = (spot == side - 1) & has_east
    carry_west = (spot == side - 1) & (plane > 0)
    carry_east = (spot == 0) & (plane < 3)

    def remote(src, dst, index, device, sender=None):
        return pltpu.make_async_remote_copy(
            src_ref=src, dst_ref=dst,
            send_sem=pair_send.at[index if sender is None else sender], recv_sem=pair_recv.at[index],
            device_id=device, device_id_type=MESH,
        )

    def when(condition, *actions):
        @pl.when(condition)
        def _():
            for action in actions:
                action()

    def scatter(src, dst, send_sem, recv_sem, peer):
        return pltpu.make_async_remote_copy(
            src_ref=src, dst_ref=dst, send_sem=send_sem, recv_sem=recv_sem,
            device_id={"col": peer}, device_id_type=MESH,
        )

    def everyone(body):
        def step(k, carry):
            body(lax.rem(c + k, cols))
            return carry

        lax.fori_loop(1, cols, step, 0)

    def half_of(index, start, body):
        def step(k, carry):
            body(index * block + lax.rem(c + k, block))
            return carry

        lax.fori_loop(start, block, step, 0)

    def arrived(buffer, sem):
        pltpu.make_async_copy(buffer, buffer, sem).wait()

    barrier = pltpu.get_barrier_semaphore()
    everyone(lambda peer: pl.semaphore_signal(barrier, inc=1, device_id={"col": peer}, device_id_type=MESH))
    for peer in (north, south):
        pl.semaphore_signal(barrier, inc=1, device_id={"row": peer}, device_id_type=MESH)

    pl.semaphore_signal(barrier, inc=1, device_id={"row": south, "col": across}, device_id_type=MESH)
    pairs = [
        (coeffs_hbm, coeffs_ref), (region_hbm, region_ref), (modes_hbm, modes_ref), (object_hbm, object_ref),
        (offsets_hbm, offsets_ref), (counts_hbm, counts_ref), (inten_hbm, inten), (m_hbm, m_ref), (mt_hbm, mt_ref),
    ]
    loads = [pltpu.make_async_copy(src, dst, local_sem.at[i]) for i, (src, dst) in enumerate(pairs)]
    for load in loads:
        load.start()
    for load in loads[:2]:
        load.wait()
    mixes[c] = jnp.zeros((SLOT_ROWS, PAD), F32)
    for p in range(slots):
        weights = coeffs_ref[0, 0, p : p + 1, :]
        area = region_ref[0, :, p : p + 1]
        mixes[c, p : p + 1, :num_modes] = jnp.where(area == r, weights, 0.0)
        mixes[c, p : p + 1, num_modes : 2 * num_modes] = jnp.where(area == r + 1, weights, 0.0)
    for load in loads[2:4]:
        load.wait()
    ext[:, inner, inner] = object_ref[...].astype(BF16)
    pl.semaphore_wait(barrier, cols + 2)

    everyone(lambda peer: scatter(mixes.at[c], mixes.at[c], mix_send, mix_recv, peer).start())
    send_modes = remote(modes_ref, nxt, 0, {"row": north})
    help_modes = remote(modes_ref, help_own, 14, {"row": r, "col": across})
    help_next = remote(modes_ref, help_nxt, 15, {"row": north, "col": across})
    help_pass = remote(help_own, help_nxt, 15, {"row": north})
    when(outer, help_modes.start)
    send_modes.start()
    when(outer & even, help_next.start)
    to_north = remote(ext.at[:, low, inner], ext.at[:, last, inner], 1, {"row": north})
    to_south = remote(ext.at[:, high, inner], ext.at[:, first, inner], 2, {"row": south})
    to_west = remote(ext.at[:, inner, low], ext.at[:, inner, last], 3, {"col": west})
    to_east = remote(ext.at[:, inner, high], ext.at[:, inner, first], 4, {"col": east})
    west_turn = remote(ext.at[:, inner, low], carried.at[0], 16, {"col": c + side - 1})
    east_turn = remote(ext.at[:, inner, high], carried.at[1], 17, {"col": c - side + 1})
    west_pass = remote(carried.at[0], ext.at[:, inner, last], 3, {"col": c - side}, 18)
    east_pass = remote(carried.at[1], ext.at[:, inner, first], 4, {"col": c + side}, 19)
    go_west, go_east = has_west & (spot > 0), has_east & (spot < side - 1)
    when(turn_west, west_turn.start)
    when(turn_east, east_turn.start)
    to_north.start()
    to_south.start()
    when(go_west, to_west.start)
    when(go_east, to_east.start)

    def stack_modes(stack, modes, start):
        for part in range(2):
            stack[start : start + split, pl.ds(part * size, size)] = modes[0, :, part].reshape(split, size)

    stack_modes(stack, modes_ref, 0)
    stack[split:] = jnp.zeros((split, full), BF16)
    help_stack[split:] = jnp.zeros((split, full), BF16)

    arrived(mixes.at[others], mix_recv)
    mixed = mixes[...].reshape(cols * SLOT_ROWS, PAD)
    coarse = mixed.astype(BF16)
    fine = (mixed - coarse.astype(F32)).astype(BF16)
    repeat = where_bf16(iota((PAD, width), 0) == lax.div(iota((PAD, width), 1), strip))
    diagonal = iota((strip, width), 0) == lax.rem(iota((strip, width), 1), strip)
    for i, part in enumerate((coarse, fine)):
        wide = dot(part, repeat).reshape(cols, SLOT_ROWS, width)
        for p in range(slots):
            spread = jnp.where(diagonal[None], wide[:, p : p + 1, :], 0.0)
            kron[i, p] = spread.reshape(size, width).astype(BF16)

    def probe_copy(share, p, index, strip_index, peer):
        return scatter(share.at[p, index], probes.at[p, strip_index], probe_send.at[p], probe_recv.at[p], peer)

    def mix_slot(p):
        both = dot(kron[0, p], stack[...]) + dot(kron[1, p], stack[...])
        for part in range(2):
            value = both[:, part * size : (part + 1) * size].astype(BF16)
            share[p, :, part] = value.reshape(cols, strip, size)
        half_of(group, 1, lambda peer: probe_copy(share, p, peer, c, peer).start())
        when(helper, lambda: half_of(1 - group, 0, lambda peer: probe_copy(share, p, peer, c, peer).start()))
        probes[p, c] = share[p, c]

    def help_slot(p):
        @pl.when(helper)
        def _():
            lines = pl.ds(pl.multiple_of(group * half, half), half)
            both = dot(kron[0, p, lines], help_stack[...]) + dot(kron[1, p, lines], help_stack[...])
            for part in range(2):
                value = both[:, part * size : (part + 1) * size].astype(BF16)
                help_share[p, :, part] = value.reshape(block, strip, size)
            half_of(group, 1, lambda peer: probe_copy(help_share, p, lax.rem(peer, block), across, peer).start())
            probes[p, across] = help_share[p, lax.rem(c, block)]

    mix_slot(0)

    @pl.when(helper)
    def _():
        help_modes.wait_recv()
        when(jnp.logical_not(even), help_pass.start)
        stack_modes(help_stack, help_own, 0)

    help_slot(0)
    send_modes.wait_recv()
    stack_modes(stack, nxt, split)
    mix_slot(1)

    @pl.when(helper)
    def _():
        help_next.wait_recv()
        stack_modes(help_stack, help_nxt, split)

    help_slot(1)
    when(carry_west, west_turn.wait_recv, west_pass.start)
    when(carry_east, east_turn.wait_recv, east_pass.start)
    to_south.wait_recv()
    north_west = remote(ext.at[:, first, low], ext.at[:, first, last], 5, {"col": west})
    north_east = remote(ext.at[:, first, high], ext.at[:, first, first], 6, {"col": east})
    when(has_west, north_west.start)
    when(has_east, north_east.start)
    to_north.wait_recv()
    south_west = remote(ext.at[:, last, low], ext.at[:, last, last], 7, {"col": west})
    south_east = remote(ext.at[:, last, high], ext.at[:, last, first], 8, {"col": east})
    when(has_west, south_west.start)
    when(has_east, south_east.start)
    for p in range(2, slots):
        mix_slot(p)
        help_slot(p)

    repeat_t = where_bf16(iota((width, PAD), 1) == lax.div(iota((width, PAD), 0), strip))
    diagonal_t = lax.rem(iota((width, size), 0), strip) == lax.rem(iota((width, size), 1), strip)
    for i, part in enumerate((coarse, fine)):
        wide_t = lax.dot_general(repeat_t, part, (((1,), (1,)), ((), ())), preferred_element_type=F32).astype(BF16)
        for p in range(slots):
            sel_shape = (cols * SLOT_ROWS, size)
            select = where_bf16(iota(sel_shape, 0) == lax.div(iota(sel_shape, 1), strip) * SLOT_ROWS + p)
            kron_t[i, p] = jnp.where(diagonal_t, dot(wide_t, select), 0.0).astype(BF16)
    acc[...] = jnp.zeros_like(acc)
    for load in loads[4:]:
        load.wait()

    when(has_east, *(copy.wait_recv for copy in (to_west, north_west, south_west)))
    when(has_west, *(copy.wait_recv for copy in (to_east, north_east, south_east)))
    for copy in (to_north, to_south):
        copy.wait_send()
    when(go_west, to_west.wait_send)
    when(go_east, to_east.wait_send)
    when(turn_west, west_turn.wait_send)
    when(turn_east, east_turn.wait_send)
    when(has_west, north_west.wait_send, south_west.wait_send)
    when(has_east, north_east.wait_send, south_east.wait_send)
    for edge, box in (
        (r == 0, (slice(None), first, slice(None))),
        (r == rows - 1, (slice(None), last, slice(None))),
        (c == 0, (slice(None), pl.ds(0, full), first)),
        (c == cols - 1, (slice(None), pl.ds(0, full), last)),
    ):

        @pl.when(edge)
        def _(box=box):
            ext[box] = jnp.zeros_like(ext[box])

    def corner(p, axis):
        return offsets_ref[0, 0, axis : axis + 1, p : p + 1] + half

    for p in range(slots):
        pick_rows = where_bf16(iota((size, full), 1) == iota((size, full), 0) + corner(p, 0))
        pick_cols = where_bf16(iota((full, size), 0) == iota((full, size), 1) + corner(p, 1))
        for plane in range(2):
            narrow = dot(ext[plane], pick_cols).astype(BF16)
            windows[p, plane] = dot(pick_rows, narrow).astype(BF16)

    def send_terms(p):
        everyone(
            lambda peer: scatter(terms.at[p, peer], got_terms.at[p, c], term_send.at[p], term_recv.at[p], peer).start()
        )
        got_terms[p, c] = terms[p, c]

    def position(p):
        when(outer, lambda: arrived(probes.at[p, others], probe_recv.at[p]))
        when(helper, lambda: arrived(probes.at[p, pl.ds(0, cols - 2)], probe_recv.at[p]))
        pr_re = probes[p, :, 0].reshape(size, size).astype(F32)
        pr_im = probes[p, :, 1].reshape(size, size).astype(F32)
        w_re = windows[p, 0].astype(F32)
        w_im = windows[p, 1].astype(F32)
        e_re = (pr_re * w_re - pr_im * w_im).astype(BF16)
        e_im = (pr_re * w_im + pr_im * w_re).astype(BF16)
        left = dot(m_ref[...], jnp.concatenate([e_re, e_im], axis=0)).astype(BF16)
        far = dot(jnp.concatenate([left[:size], left[size:]], axis=1), mt_ref[...])
        f_re, f_im = far[:, :size], far[:, size:]
        energy = jnp.maximum(f_re * f_re + f_im * f_im, FLOOR * FLOOR)
        live = jnp.where(counts_ref[...] > p, 1.0, 0.0)
        factor = (jnp.sqrt(inten[0, 0, p].astype(F32)) * lax.rsqrt(energy) - 1.0) * live
        c_re = (f_re * factor).astype(BF16)
        c_im = (f_im * factor).astype(BF16)
        back = dot(mt_ref[...], jnp.concatenate([c_re, c_im], axis=0)).astype(BF16)
        update = dot(jnp.concatenate([back[:size], back[size:]], axis=1), m_ref[...])
        u_re, u_im = update[:, :size], update[:, size:]
        terms[p, :, 0] = (w_re * u_re + w_im * u_im).astype(BF16).reshape(cols, strip, size)
        terms[p, :, 1] = (w_re * u_im - w_im * u_re).astype(BF16).reshape(cols, strip, size)
        if p < slots - 1:
            send_terms(p)
        put_rows = where_bf16(iota((full, size), 0) == iota((full, size), 1) + corner(p, 0))
        put_cols = where_bf16(iota((size, full), 1) == iota((size, full), 0) + corner(p, 1))
        for plane, value in enumerate((pr_re * u_re + pr_im * u_im, pr_re * u_im - pr_im * u_re)):
            acc[plane] += dot(put_rows, dot(value.astype(BF16), put_cols).astype(BF16))

    for p in range(slots):
        position(p)

    out_cols[0] = acc[:, :, first].astype(BF16)
    out_cols[1] = acc[:, :, last].astype(BF16)
    top, bottom = pl.ds(0, size), pl.ds(size, size)
    cols_west = [remote(out_cols.at[0, :, rows_of], got_cols.at[1, :, rows_of], i, {"col": west})
                 for i, rows_of in ((9, top), (20, bottom))]
    cols_east = [remote(out_cols.at[1, :, rows_of], got_cols.at[0, :, rows_of], i, {"col": east})
                 for i, rows_of in ((10, top), (21, bottom))]
    west_turn_out = remote(out_cols.at[0, :, top], carried_out.at[0], 22, {"col": c + side - 1})
    east_turn_out = remote(out_cols.at[1, :, top], carried_out.at[1], 23, {"col": c - side + 1})
    west_pass_out = remote(carried_out.at[0], got_cols.at[1, :, top], 9, {"col": c - side}, 24)
    east_pass_out = remote(carried_out.at[1], got_cols.at[0, :, top], 10, {"col": c + side}, 25)
    when(turn_west, west_turn_out.start)
    when(turn_east, east_turn_out.start)
    when(go_west, cols_west[0].start)
    when(go_east, cols_east[0].start)
    when(has_west, cols_west[1].start)
    when(has_east, cols_east[1].start)
    send_terms(slots - 1)

    def gather(p, part_of):
        both = jnp.concatenate([got_terms[p, :, plane].reshape(size, size) for plane in range(2)], axis=1)
        where = pl.ds(part_of * split, split)
        value = dot(kron_t[0, p, where], both) + dot(kron_t[1, p, where], both)
        if p == 0:
            sums[where] = value
        else:
            sums[where] += value

    arrived(got_terms.at[0, others], term_recv.at[0])
    gather(0, 1)
    when(carry_west, west_turn_out.wait_recv, west_pass_out.start)
    when(carry_east, east_turn_out.wait_recv, east_pass_out.start)
    for p in range(1, slots - 2):
        arrived(got_terms.at[p, others], term_recv.at[p])
        gather(p, 1)

    when(has_west, *(copy.wait_recv for copy in cols_east))
    acc[:, :, low] += jnp.where(c == 0, 0.0, got_cols[0].astype(F32))
    when(has_east, *(copy.wait_recv for copy in cols_west))
    acc[:, :, high] += jnp.where(c == cols - 1, 0.0, got_cols[1].astype(F32))
    out_rows[0] = acc[:, first, inner].astype(BF16)
    out_rows[1] = acc[:, last, inner].astype(BF16)
    rows_north = remote(out_rows.at[0], got_rows.at[1], 11, {"row": north})
    rows_south = remote(out_rows.at[1], got_rows.at[0], 12, {"row": south})
    rows_north.start()
    rows_south.start()

    for p in range(slots - 2, slots):
        arrived(got_terms.at[p, others], term_recv.at[p])
        gather(p, 1)
    for plane in range(2):
        part = sums[split:, pl.ds(plane * size, size)].astype(BF16)
        out_sums[:, plane] = part.reshape(num_modes, strip, size)
    send_sums = remote(out_sums, got_sums, 13, {"row": south})
    send_sums.start()
    for p in range(slots):
        gather(p, 0)

    rows_south.wait_recv()
    grad_ref[:, pl.ds(0, half), :] = acc[:, low, inner] + jnp.where(r == 0, 0.0, got_rows[0].astype(F32))
    rows_north.wait_recv()
    grad_ref[:, pl.ds(half, half), :] = acc[:, high, inner] + jnp.where(r == rows - 1, 0.0, got_rows[1].astype(F32))
    send_sums.wait_recv()
    for plane in range(2):
        own = sums[:split, pl.ds(plane * size, size)].reshape(num_modes, strip, size)
        mode_ref[0, :, plane] = own + got_sums[:, plane].astype(F32)

    for copy in (send_modes, rows_north, rows_south, send_sums):
        copy.wait_send()
    when(outer, help_modes.wait_send)
    when(outer & even, help_next.wait_send)
    when(helper & jnp.logical_not(even), help_pass.wait_send)
    when(carry_west, west_pass.wait_send, west_pass_out.wait_send)
    when(carry_east, east_pass.wait_send, east_pass_out.wait_send)
    when(turn_west, west_turn_out.wait_send)
    when(turn_east, east_turn_out.wait_send)
    when(go_west, cols_west[0].wait_send)
    when(go_east, cols_east[0].wait_send)
    when(has_west, cols_west[1].wait_send)
    when(has_east, cols_east[1].wait_send)
    arrived(mixes.at[others], mix_send)
    for p in range(slots):
        near = pl.ds(0, block - 1)
        arrived(share.at[p, near], probe_send.at[p])
        when(helper, lambda p=p: arrived(share.at[p, pl.ds(0, block)], probe_send.at[p]))
        when(helper, lambda p=p: arrived(help_share.at[p, near], probe_send.at[p]))
        arrived(terms.at[p, others], term_send.at[p])


def local(object_field, modes, coeffs, offsets, region, counts, intensity):
    size = modes.shape[-1]
    half = size // 2
    full = 2 * size
    num_modes = modes.shape[1]
    slots = coeffs.shape[2]
    strip = modes.shape[3]
    rows, cols = lax.axis_size("row"), lax.axis_size("col")
    block, block_t = dft_blocks(size)
    width = 2 * num_modes * strip
    vmem = pl.BlockSpec(memory_space=pltpu.VMEM)
    hbm = pl.BlockSpec(memory_space=pl.ANY)
    pieces = (slots, cols, 2, strip, size)
    dma = pltpu.SemaphoreType.DMA
    args = (
        object_field, modes, coeffs, jnp.swapaxes(offsets, 2, 3), region, counts, intensity, jnp.asarray(block), jnp.asarray(block_t),
    )
    return pl.pallas_call(
        functools.partial(kernel, (rows, cols, slots, num_modes, strip)),
        out_shape=(
            jax.ShapeDtypeStruct((2, size, size), F32),
            jax.ShapeDtypeStruct((1, num_modes, 2, strip, size), F32),
        ),
        in_specs=[hbm] * len(args),
        out_specs=(vmem, vmem),
        scratch_shapes=[pltpu.VMEM(x.shape, x.dtype) for x in args]
        + [
            pltpu.VMEM((2, full, full), BF16),
            pltpu.VMEM(modes.shape, BF16),
            pltpu.VMEM((cols, SLOT_ROWS, PAD), F32),
            pltpu.VMEM((width, full), BF16),
            pltpu.VMEM((2, slots, size, width), BF16),
            pltpu.VMEM((2, slots, width, size), BF16),
            pltpu.VMEM(pieces, BF16),
            pltpu.VMEM(pieces, BF16),
            pltpu.VMEM((slots, 2, size, size), BF16),
            pltpu.VMEM(modes.shape, BF16),
            pltpu.VMEM(modes.shape, BF16),
            pltpu.VMEM((width, full), BF16),
            pltpu.VMEM((slots, cols // 2, 2, strip, size), BF16),
            pltpu.VMEM((2, 2, size, half), BF16),
            pltpu.VMEM((2, 2, size, half), BF16),
            pltpu.VMEM(pieces, BF16),
            pltpu.VMEM(pieces, BF16),
            pltpu.VMEM((2, full, full), F32),
            pltpu.VMEM((2, 2, full, half), BF16),
            pltpu.VMEM((2, 2, full, half), BF16),
            pltpu.VMEM((2, 2, half, size), BF16),
            pltpu.VMEM((2, 2, half, size), BF16),
            pltpu.VMEM((width, full), F32),
            pltpu.VMEM((num_modes, 2, strip, size), BF16),
            pltpu.VMEM((num_modes, 2, strip, size), BF16),
            dma((len(args),)),
            dma((26,)),
            dma((26,)),
            dma,
            dma,
            dma((slots,)),
            dma((slots,)),
            dma((slots,)),
            dma((slots,)),
        ],
        compiler_params=pltpu.CompilerParams(
            collective_id=0, has_side_effects=True, vmem_limit_bytes=56 << 20
        ),
        name="ptychography",
    )(*args)


def solution(mesh):
    in_specs = (
        P(None, "row", "col"),
        P("row", None, None, "col", None),
        P("row", "col", None, None),
        P("row", "col", None, None),
        P("row", "col", None),
        P("row", "col"),
        P("row", "col", None, None, None),
    )
    out_specs = (P(None, "row", "col"), P("row", None, None, "col", None))
    return jax.shard_map(local, mesh=mesh, in_specs=in_specs, out_specs=out_specs, check_vma=False)
```

```python
import functools
import math

import jax
import jax.numpy as jnp
import numpy as np
from jax import lax
from jax.experimental import pallas as pl
from jax.experimental.pallas import tpu as pltpu
from jax.sharding import PartitionSpec as P

FLOOR = 0.25
PAD = 128
SLOT_ROWS = 8
F32 = jnp.float32
BF16 = jnp.bfloat16
MESH = pl.DeviceIdType.MESH


def dft_blocks(length):
    index = np.arange(length)
    angles = (index[:, None] * index[None, :] % length).astype(np.float32) * np.float32(2.0 * math.pi / length)
    scaling = np.float32(1.0 / math.sqrt(length))
    re = (np.cos(angles) * scaling).astype(jnp.bfloat16)
    im = (-np.sin(angles) * scaling).astype(jnp.bfloat16)
    block = np.block([[re, -im], [im, re]])
    return block, np.ascontiguousarray(block.T)


def dot(a, b):
    return jnp.dot(a, b, preferred_element_type=F32)


def iota(shape, dim):
    return lax.broadcasted_iota(jnp.int32, shape, dim)


def where_bf16(mask):
    return jnp.where(mask, 1.0, 0.0).astype(BF16)


def kernel(
    dims,
    object_hbm, modes_hbm, coeffs_hbm, offsets_hbm, region_hbm, counts_hbm, inten_hbm, m_hbm, mt_hbm,
    grad_ref, mode_ref,
    object_ref, modes_ref, coeffs_ref, offsets_ref, region_ref, counts_ref, inten, m_ref, mt_ref,
    ext, nxt, mixes, stack, kron, kron_t, share, probes, windows,
    help_own, help_nxt, help_stack, help_share, carried, carried_out,
    terms, got_terms, got_help, help_sums, out_help, in_help, acc, out_cols, got_cols, out_rows, got_rows, sums, out_sums, got_sums,
    local_sem, pair_send, pair_recv, mix_send, mix_recv, probe_send, probe_recv, term_send, term_recv, help_recv,
):
    rows, cols, slots, num_modes, strip = dims
    size = cols * strip
    half = size // 2
    full = 2 * size
    split = num_modes * strip
    width = 2 * split
    r, c = lax.axis_index("row"), lax.axis_index("col")
    north, south = lax.rem(r + rows - 1, rows), lax.rem(r + 1, rows)
    west, east = lax.rem(c + cols - 1, cols), lax.rem(c + 1, cols)
    inner = pl.ds(half, size)
    low, high = pl.ds(half, half), pl.ds(size, half)
    first, last = pl.ds(0, half), pl.ds(size + half, half)
    others = pl.ds(0, cols - 1)
    side = cols // 4
    block = cols // 2
    plane, spot = lax.div(c, side), lax.rem(c, side)
    group = lax.div(c, block)
    outer = (plane == 0) | (plane == 3)
    helper = (plane == 1) | (plane == 2)
    across = lax.rem(c + block, cols)
    even = lax.rem(r, 2) == 0
    has_west, has_east = c > 0, c < cols - 1
    turn_west = (spot == 0) & has_west
    turn_east = (spot == side - 1) & has_east
    carry_west = (spot == side - 1) & (plane > 0)
    carry_east = (spot == 0) & (plane < 3)

    def remote(src, dst, index, device, sender=None):
        return pltpu.make_async_remote_copy(
            src_ref=src, dst_ref=dst,
            send_sem=pair_send.at[index if sender is None else sender], recv_sem=pair_recv.at[index],
            device_id=device, device_id_type=MESH,
        )

    def when(condition, *actions):
        @pl.when(condition)
        def _():
            for action in actions:
                action()

    def scatter(src, dst, send_sem, recv_sem, peer):
        return pltpu.make_async_remote_copy(
            src_ref=src, dst_ref=dst, send_sem=send_sem, recv_sem=recv_sem,
            device_id={"col": peer}, device_id_type=MESH,
        )

    def everyone(body):
        def step(k, carry):
            body(lax.rem(c + k, cols))
            return carry

        lax.fori_loop(1, cols, step, 0)

    def half_of(index, start, body):
        def step(k, carry):
            body(index * block + lax.rem(c + k, block))
            return carry

        lax.fori_loop(start, block, step, 0)

    def arrived(buffer, sem):
        pltpu.make_async_copy(buffer, buffer, sem).wait()

    barrier = pltpu.get_barrier_semaphore()
    everyone(lambda peer: pl.semaphore_signal(barrier, inc=1, device_id={"col": peer}, device_id_type=MESH))
    for peer in (north, south):
        pl.semaphore_signal(barrier, inc=1, device_id={"row": peer}, device_id_type=MESH)

    for peer in (north, south):
        pl.semaphore_signal(barrier, inc=1, device_id={"row": peer, "col": across}, device_id_type=MESH)
    pairs = [
        (coeffs_hbm, coeffs_ref), (region_hbm, region_ref), (modes_hbm, modes_ref), (object_hbm, object_ref),
        (offsets_hbm, offsets_ref), (counts_hbm, counts_ref), (inten_hbm, inten), (m_hbm, m_ref), (mt_hbm, mt_ref),
    ]
    loads = [pltpu.make_async_copy(src, dst, local_sem.at[i]) for i, (src, dst) in enumerate(pairs)]
    for load in loads:
        load.start()
    for load in loads[:2]:
        load.wait()
    mixes[c] = jnp.zeros((SLOT_ROWS, PAD), F32)
    for p in range(slots):
        weights = coeffs_ref[0, 0, p : p + 1, :]
        area = region_ref[0, :, p : p + 1]
        mixes[c, p : p + 1, :num_modes] = jnp.where(area == r, weights, 0.0)
        mixes[c, p : p + 1, num_modes : 2 * num_modes] = jnp.where(area == r + 1, weights, 0.0)
    for load in loads[2:4]:
        load.wait()
    ext[:, inner, inner] = object_ref[...].astype(BF16)
    pl.semaphore_wait(barrier, cols + 3)

    everyone(lambda peer: scatter(mixes.at[c], mixes.at[c], mix_send, mix_recv, peer).start())
    send_modes = remote(modes_ref, nxt, 0, {"row": north})
    help_modes = remote(modes_ref, help_own, 14, {"row": r, "col": across})
    help_next = remote(modes_ref, help_nxt, 15, {"row": north, "col": across})
    help_pass = remote(help_own, help_nxt, 15, {"row": north})
    when(outer, help_modes.start)
    send_modes.start()
    when(outer & even, help_next.start)
    to_north = remote(ext.at[:, low, inner], ext.at[:, last, inner], 1, {"row": north})
    to_south = remote(ext.at[:, high, inner], ext.at[:, first, inner], 2, {"row": south})
    to_west = remote(ext.at[:, inner, low], ext.at[:, inner, last], 3, {"col": west})
    to_east = remote(ext.at[:, inner, high], ext.at[:, inner, first], 4, {"col": east})
    west_turn = remote(ext.at[:, inner, low], carried.at[0], 16, {"col": c + side - 1})
    east_turn = remote(ext.at[:, inner, high], carried.at[1], 17, {"col": c - side + 1})
    west_pass = remote(carried.at[0], ext.at[:, inner, last], 3, {"col": c - side}, 18)
    east_pass = remote(carried.at[1], ext.at[:, inner, first], 4, {"col": c + side}, 19)
    go_west, go_east = has_west & (spot > 0), has_east & (spot < side - 1)
    when(turn_west, west_turn.start)
    when(turn_east, east_turn.start)
    to_north.start()
    to_south.start()
    when(go_west, to_west.start)
    when(go_east, to_east.start)

    def stack_modes(stack, modes, start):
        for part in range(2):
            stack[start : start + split, pl.ds(part * size, size)] = modes[0, :, part].reshape(split, size)

    stack_modes(stack, modes_ref, 0)
    stack[split:] = jnp.zeros((split, full), BF16)
    help_stack[split:] = jnp.zeros((split, full), BF16)

    arrived(mixes.at[others], mix_recv)
    mixed = mixes[...].reshape(cols * SLOT_ROWS, PAD)
    coarse = mixed.astype(BF16)
    fine = (mixed - coarse.astype(F32)).astype(BF16)
    repeat = where_bf16(iota((PAD, width), 0) == lax.div(iota((PAD, width), 1), strip))
    diagonal = iota((strip, width), 0) == lax.rem(iota((strip, width), 1), strip)
    for i, part in enumerate((coarse, fine)):
        wide = dot(part, repeat).reshape(cols, SLOT_ROWS, width)
        for p in range(slots):
            spread = jnp.where(diagonal[None], wide[:, p : p + 1, :], 0.0)
            kron[i, p] = spread.reshape(size, width).astype(BF16)

    def probe_copy(share, p, index, strip_index, peer):
        return scatter(share.at[p, index], probes.at[p, strip_index], probe_send.at[p], probe_recv.at[p], peer)

    def mix_slot(p):
        both = dot(kron[0, p], stack[...]) + dot(kron[1, p], stack[...])
        for part in range(2):
            value = both[:, part * size : (part + 1) * size].astype(BF16)
            share[p, :, part] = value.reshape(cols, strip, size)
        half_of(group, 1, lambda peer: probe_copy(share, p, peer, c, peer).start())
        when(helper, lambda: half_of(1 - group, 0, lambda peer: probe_copy(share, p, peer, c, peer).start()))
        probes[p, c] = share[p, c]

    def help_slot(p):
        @pl.when(helper)
        def _():
            lines = pl.ds(pl.multiple_of(group * half, half), half)
            both = dot(kron[0, p, lines], help_stack[...]) + dot(kron[1, p, lines], help_stack[...])
            for part in range(2):
                value = both[:, part * size : (part + 1) * size].astype(BF16)
                help_share[p, :, part] = value.reshape(block, strip, size)
            half_of(group, 1, lambda peer: probe_copy(help_share, p, lax.rem(peer, block), across, peer).start())
            probes[p, across] = help_share[p, lax.rem(c, block)]

    mix_slot(0)

    @pl.when(helper)
    def _():
        help_modes.wait_recv()
        when(jnp.logical_not(even), help_pass.start)
        stack_modes(help_stack, help_own, 0)

    help_slot(0)
    send_modes.wait_recv()
    stack_modes(stack, nxt, split)
    mix_slot(1)

    @pl.when(helper)
    def _():
        help_next.wait_recv()
        stack_modes(help_stack, help_nxt, split)

    help_slot(1)
    when(carry_west, west_turn.wait_recv, west_pass.start)
    when(carry_east, east_turn.wait_recv, east_pass.start)
    to_south.wait_recv()
    north_west = remote(ext.at[:, first, low], ext.at[:, first, last], 5, {"col": west})
    north_east = remote(ext.at[:, first, high], ext.at[:, first, first], 6, {"col": east})
    when(has_west, north_west.start)
    when(has_east, north_east.start)
    to_north.wait_recv()
    south_west = remote(ext.at[:, last, low], ext.at[:, last, last], 7, {"col": west})
    south_east = remote(ext.at[:, last, high], ext.at[:, last, first], 8, {"col": east})
    when(has_west, south_west.start)
    when(has_east, south_east.start)
    for p in range(2, slots):
        mix_slot(p)
        help_slot(p)

    repeat_t = where_bf16(iota((width, PAD), 1) == lax.div(iota((width, PAD), 0), strip))
    diagonal_t = lax.rem(iota((width, size), 0), strip) == lax.rem(iota((width, size), 1), strip)
    for i, part in enumerate((coarse, fine)):
        wide_t = lax.dot_general(repeat_t, part, (((1,), (1,)), ((), ())), preferred_element_type=F32).astype(BF16)
        for p in range(slots):
            sel_shape = (cols * SLOT_ROWS, size)
            select = where_bf16(iota(sel_shape, 0) == lax.div(iota(sel_shape, 1), strip) * SLOT_ROWS + p)
            kron_t[i, p] = jnp.where(diagonal_t, dot(wide_t, select), 0.0).astype(BF16)
    acc[...] = jnp.zeros_like(acc)

    @pl.when(outer)
    def _():
        got_terms[:, pl.ds((1 - group) * block, block)] = jnp.zeros((slots, block, 2, strip, size), BF16)

    for load in loads[4:]:
        load.wait()

    when(has_east, *(copy.wait_recv for copy in (to_west, north_west, south_west)))
    when(has_west, *(copy.wait_recv for copy in (to_east, north_east, south_east)))
    for copy in (to_north, to_south):
        copy.wait_send()
    when(go_west, to_west.wait_send)
    when(go_east, to_east.wait_send)
    when(turn_west, west_turn.wait_send)
    when(turn_east, east_turn.wait_send)
    when(has_west, north_west.wait_send, south_west.wait_send)
    when(has_east, north_east.wait_send, south_east.wait_send)
    for edge, box in (
        (r == 0, (slice(None), first, slice(None))),
        (r == rows - 1, (slice(None), last, slice(None))),
        (c == 0, (slice(None), pl.ds(0, full), first)),
        (c == cols - 1, (slice(None), pl.ds(0, full), last)),
    ):

        @pl.when(edge)
        def _(box=box):
            ext[box] = jnp.zeros_like(ext[box])

    def corner(p, axis):
        return offsets_ref[0, 0, axis : axis + 1, p : p + 1] + half

    for p in range(slots):
        pick_rows = where_bf16(iota((size, full), 1) == iota((size, full), 0) + corner(p, 0))
        pick_cols = where_bf16(iota((full, size), 0) == iota((full, size), 1) + corner(p, 1))
        for plane in range(2):
            narrow = dot(ext[plane], pick_cols).astype(BF16)
            windows[p, plane] = dot(pick_rows, narrow).astype(BF16)

    def send_terms(p):
        def direct(peer):
            scatter(terms.at[p, peer], got_terms.at[p, c], term_send.at[p], term_recv.at[p], peer).start()

        def helped(k):
            target = (3 - 3 * group) * side + lax.rem(c + k, side)
            spot_of = got_help.at[p, lax.rem(c, block)]
            scatter(terms.at[p, target], spot_of, term_send.at[p], help_recv.at[p], lax.rem(target + block, cols)).start()

        def step(k, carry):
            direct((2 - group) * side + lax.rem(c + k, side))
            return carry

        def help_step(k, carry):
            helped(k)
            return carry

        lax.fori_loop(0, side, step, 0)
        when(outer, lambda: helped(0))
        lax.fori_loop(1, side, help_step, 0)
        half_of(group, 1, direct)
        got_terms[p, c] = terms[p, c]

        @pl.when(helper)
        def _():
            got_help[p, lax.rem(c, block)] = terms[p, across]

    def terms_here(p):
        when(outer, lambda: arrived(got_terms.at[p, pl.ds(0, block - 1)], term_recv.at[p]))
        when(helper, lambda: arrived(got_terms.at[p, others], term_recv.at[p]))

    def gather_help(p):
        @pl.when(helper)
        def _():
            arrived(got_help.at[p, pl.ds(0, block - 1)], help_recv.at[p])
            both = jnp.concatenate([got_help[p, :, part].reshape(half, size) for part in range(2)], axis=1)
            lanes = pl.ds(pl.multiple_of(group * half, half), half)
            value = dot(kron_t[0, p, :, lanes], both) + dot(kron_t[1, p, :, lanes], both)
            if p == 0:
                help_sums[...] = value
            else:
                help_sums[...] += value

    def position(p):
        when(outer, lambda: arrived(probes.at[p, others], probe_recv.at[p]))
        when(helper, lambda: arrived(probes.at[p, pl.ds(0, cols - 2)], probe_recv.at[p]))
        pr_re = probes[p, :, 0].reshape(size, size).astype(F32)
        pr_im = probes[p, :, 1].reshape(size, size).astype(F32)
        w_re = windows[p, 0].astype(F32)
        w_im = windows[p, 1].astype(F32)
        e_re = (pr_re * w_re - pr_im * w_im).astype(BF16)
        e_im = (pr_re * w_im + pr_im * w_re).astype(BF16)
        left = dot(m_ref[...], jnp.concatenate([e_re, e_im], axis=0)).astype(BF16)
        far = dot(jnp.concatenate([left[:size], left[size:]], axis=1), mt_ref[...])
        f_re, f_im = far[:, :size], far[:, size:]
        energy = jnp.maximum(f_re * f_re + f_im * f_im, FLOOR * FLOOR)
        live = jnp.where(counts_ref[...] > p, 1.0, 0.0)
        factor = (jnp.sqrt(inten[0, 0, p].astype(F32)) * lax.rsqrt(energy) - 1.0) * live
        c_re = (f_re * factor).astype(BF16)
        c_im = (f_im * factor).astype(BF16)
        back = dot(mt_ref[...], jnp.concatenate([c_re, c_im], axis=0)).astype(BF16)
        update = dot(jnp.concatenate([back[:size], back[size:]], axis=1), m_ref[...])
        u_re, u_im = update[:, :size], update[:, size:]
        terms[p, :, 0] = (w_re * u_re + w_im * u_im).astype(BF16).reshape(cols, strip, size)
        terms[p, :, 1] = (w_re * u_im - w_im * u_re).astype(BF16).reshape(cols, strip, size)
        if p < slots - 1:
            send_terms(p)
        put_rows = where_bf16(iota((full, size), 0) == iota((full, size), 1) + corner(p, 0))
        put_cols = where_bf16(iota((size, full), 1) == iota((size, full), 0) + corner(p, 1))
        for plane, value in enumerate((pr_re * u_re + pr_im * u_im, pr_re * u_im - pr_im * u_re)):
            acc[plane] += dot(put_rows, dot(value.astype(BF16), put_cols).astype(BF16))

    for p in range(slots):
        position(p)

    out_cols[0] = acc[:, :, first].astype(BF16)
    out_cols[1] = acc[:, :, last].astype(BF16)
    top, bottom = pl.ds(0, size), pl.ds(size, size)
    cols_west = [remote(out_cols.at[0, :, rows_of], got_cols.at[1, :, rows_of], i, {"col": west})
                 for i, rows_of in ((9, top), (20, bottom))]
    cols_east = [remote(out_cols.at[1, :, rows_of], got_cols.at[0, :, rows_of], i, {"col": east})
                 for i, rows_of in ((10, top), (21, bottom))]
    west_turn_out = remote(out_cols.at[0, :, top], carried_out.at[0], 22, {"col": c + side - 1})
    east_turn_out = remote(out_cols.at[1, :, top], carried_out.at[1], 23, {"col": c - side + 1})
    west_pass_out = remote(carried_out.at[0], got_cols.at[1, :, top], 9, {"col": c - side}, 24)
    east_pass_out = remote(carried_out.at[1], got_cols.at[0, :, top], 10, {"col": c + side}, 25)
    when(turn_west, west_turn_out.start)
    when(turn_east, east_turn_out.start)
    when(go_west, cols_west[0].start)
    when(go_east, cols_east[0].start)
    when(has_west, cols_west[1].start)
    when(has_east, cols_east[1].start)
    send_terms(slots - 1)

    def gather(p, part_of):
        both = jnp.concatenate([got_terms[p, :, plane].reshape(size, size) for plane in range(2)], axis=1)
        where = pl.ds(part_of * split, split)
        value = dot(kron_t[0, p, where], both) + dot(kron_t[1, p, where], both)
        if p == 0:
            sums[where] = value
        else:
            sums[where] += value

    terms_here(0)
    gather(0, 1)
    gather_help(0)
    when(carry_west, west_turn_out.wait_recv, west_pass_out.start)
    when(carry_east, east_turn_out.wait_recv, east_pass_out.start)
    for p in range(1, slots - 2):
        terms_here(p)
        gather(p, 1)
        gather_help(p)

    when(has_west, *(copy.wait_recv for copy in cols_east))
    acc[:, :, low] += jnp.where(c == 0, 0.0, got_cols[0].astype(F32))
    when(has_east, *(copy.wait_recv for copy in cols_west))
    acc[:, :, high] += jnp.where(c == cols - 1, 0.0, got_cols[1].astype(F32))
    out_rows[0] = acc[:, first, inner].astype(BF16)
    out_rows[1] = acc[:, last, inner].astype(BF16)
    rows_north = remote(out_rows.at[0], got_rows.at[1], 11, {"row": north})
    rows_south = remote(out_rows.at[1], got_rows.at[0], 12, {"row": south})
    rows_north.start()
    rows_south.start()

    for p in range(slots - 2, slots):
        gather_help(p)
    help_back = remote(out_help.at[0], in_help.at[0], 26, {"row": r, "col": across})
    help_down = remote(out_help.at[1], in_help.at[1], 27, {"row": south, "col": across})

    @pl.when(helper)
    def _():
        for i in range(2):
            for part in range(2):
                value = help_sums[i * split : (i + 1) * split, pl.ds(part * size, size)].astype(BF16)
                out_help[i, :, part] = value.reshape(num_modes, strip, size)
        help_back.start()
        help_down.start()

    for p in range(slots - 2, slots):
        terms_here(p)
        gather(p, 1)
    for plane in range(2):
        part = sums[split:, pl.ds(plane * size, size)].astype(BF16)
        out_sums[:, plane] = part.reshape(num_modes, strip, size)
    send_sums = remote(out_sums, got_sums, 13, {"row": south})
    send_sums.start()
    for p in range(slots):
        gather(p, 0)

    rows_south.wait_recv()
    grad_ref[:, pl.ds(0, half), :] = acc[:, low, inner] + jnp.where(r == 0, 0.0, got_rows[0].astype(F32))
    rows_north.wait_recv()
    grad_ref[:, pl.ds(half, half), :] = acc[:, high, inner] + jnp.where(r == rows - 1, 0.0, got_rows[1].astype(F32))
    send_sums.wait_recv()
    when(outer, help_back.wait_recv, help_down.wait_recv)
    for part in range(2):
        own = sums[:split, pl.ds(part * size, size)].reshape(num_modes, strip, size)
        extra = in_help[0, :, part].astype(F32) + in_help[1, :, part].astype(F32)
        mode_ref[0, :, part] = own + got_sums[:, part].astype(F32) + jnp.where(outer, extra, 0.0)

    when(helper, help_back.wait_send, help_down.wait_send)

    for copy in (send_modes, rows_north, rows_south, send_sums):
        copy.wait_send()
    when(outer, help_modes.wait_send)
    when(outer & even, help_next.wait_send)
    when(helper & jnp.logical_not(even), help_pass.wait_send)
    when(carry_west, west_pass.wait_send, west_pass_out.wait_send)
    when(carry_east, east_pass.wait_send, east_pass_out.wait_send)
    when(turn_west, west_turn_out.wait_send)
    when(turn_east, east_turn_out.wait_send)
    when(go_west, cols_west[0].wait_send)
    when(go_east, cols_east[0].wait_send)
    when(has_west, cols_west[1].wait_send)
    when(has_east, cols_east[1].wait_send)
    arrived(mixes.at[others], mix_send)
    for p in range(slots):
        near = pl.ds(0, block - 1)
        arrived(share.at[p, near], probe_send.at[p])
        when(helper, lambda p=p: arrived(share.at[p, pl.ds(0, block)], probe_send.at[p]))
        when(helper, lambda p=p: arrived(help_share.at[p, near], probe_send.at[p]))
        when(outer, lambda p=p: arrived(terms.at[p, others], term_send.at[p]))
        when(helper, lambda p=p: arrived(terms.at[p, pl.ds(0, cols - 2)], term_send.at[p]))


def local(object_field, modes, coeffs, offsets, region, counts, intensity):
    size = modes.shape[-1]
    half = size // 2
    full = 2 * size
    num_modes = modes.shape[1]
    slots = coeffs.shape[2]
    strip = modes.shape[3]
    rows, cols = lax.axis_size("row"), lax.axis_size("col")
    block, block_t = dft_blocks(size)
    width = 2 * num_modes * strip
    vmem = pl.BlockSpec(memory_space=pltpu.VMEM)
    hbm = pl.BlockSpec(memory_space=pl.ANY)
    pieces = (slots, cols, 2, strip, size)
    dma = pltpu.SemaphoreType.DMA
    args = (
        object_field, modes, coeffs, jnp.swapaxes(offsets, 2, 3), region, counts, intensity, jnp.asarray(block), jnp.asarray(block_t),
    )
    return pl.pallas_call(
        functools.partial(kernel, (rows, cols, slots, num_modes, strip)),
        out_shape=(
            jax.ShapeDtypeStruct((2, size, size), F32),
            jax.ShapeDtypeStruct((1, num_modes, 2, strip, size), F32),
        ),
        in_specs=[hbm] * len(args),
        out_specs=(vmem, vmem),
        scratch_shapes=[pltpu.VMEM(x.shape, x.dtype) for x in args]
        + [
            pltpu.VMEM((2, full, full), BF16),
            pltpu.VMEM(modes.shape, BF16),
            pltpu.VMEM((cols, SLOT_ROWS, PAD), F32),
            pltpu.VMEM((width, full), BF16),
            pltpu.VMEM((2, slots, size, width), BF16),
            pltpu.VMEM((2, slots, width, size), BF16),
            pltpu.VMEM(pieces, BF16),
            pltpu.VMEM(pieces, BF16),
            pltpu.VMEM((slots, 2, size, size), BF16),
            pltpu.VMEM(modes.shape, BF16),
            pltpu.VMEM(modes.shape, BF16),
            pltpu.VMEM((width, full), BF16),
            pltpu.VMEM((slots, cols // 2, 2, strip, size), BF16),
            pltpu.VMEM((2, 2, size, half), BF16),
            pltpu.VMEM((2, 2, size, half), BF16),
            pltpu.VMEM(pieces, BF16),
            pltpu.VMEM(pieces, BF16),
            pltpu.VMEM((slots, cols // 2, 2, strip, size), BF16),
            pltpu.VMEM((width, full), F32),
            pltpu.VMEM((2, num_modes, 2, strip, size), BF16),
            pltpu.VMEM((2, num_modes, 2, strip, size), BF16),
            pltpu.VMEM((2, full, full), F32),
            pltpu.VMEM((2, 2, full, half), BF16),
            pltpu.VMEM((2, 2, full, half), BF16),
            pltpu.VMEM((2, 2, half, size), BF16),
            pltpu.VMEM((2, 2, half, size), BF16),
            pltpu.VMEM((width, full), F32),
            pltpu.VMEM((num_modes, 2, strip, size), BF16),
            pltpu.VMEM((num_modes, 2, strip, size), BF16),
            dma((len(args),)),
            dma((28,)),
            dma((28,)),
            dma,
            dma,
            dma((slots,)),
            dma((slots,)),
            dma((slots,)),
            dma((slots,)),
            dma((slots,)),
        ],
        compiler_params=pltpu.CompilerParams(
            collective_id=0, has_side_effects=True, vmem_limit_bytes=56 << 20
        ),
        name="ptychography",
    )(*args)


def solution(mesh):
    in_specs = (
        P(None, "row", "col"),
        P("row", None, None, "col", None),
        P("row", "col", None, None),
        P("row", "col", None, None),
        P("row", "col", None),
        P("row", "col"),
        P("row", "col", None, None, None),
    )
    out_specs = (P(None, "row", "col"), P("row", None, None, "col", None))
    return jax.shard_map(local, mesh=mesh, in_specs=in_specs, out_specs=out_specs, check_vma=False)
```

```python
import functools
import math

import jax
import jax.numpy as jnp
import numpy as np
from jax import lax
from jax.experimental import pallas as pl
from jax.experimental.pallas import tpu as pltpu
from jax.sharding import PartitionSpec as P

FLOOR = 0.25
PAD = 128
SLOT_ROWS = 8
F32 = jnp.float32
BF16 = jnp.bfloat16
MESH = pl.DeviceIdType.MESH


def dft_blocks(length):
    index = np.arange(length)
    angles = (index[:, None] * index[None, :] % length).astype(np.float32) * np.float32(2.0 * math.pi / length)
    scaling = np.float32(1.0 / math.sqrt(length))
    re = (np.cos(angles) * scaling).astype(jnp.bfloat16)
    im = (-np.sin(angles) * scaling).astype(jnp.bfloat16)
    block = np.block([[re, -im], [im, re]])
    return block, np.ascontiguousarray(block.T)


def dot(a, b):
    return jnp.dot(a, b, preferred_element_type=F32)


def iota(shape, dim):
    return lax.broadcasted_iota(jnp.int32, shape, dim)


def where_bf16(mask):
    return jnp.where(mask, 1.0, 0.0).astype(BF16)


def kernel(
    dims,
    object_hbm, modes_hbm, coeffs_hbm, offsets_hbm, region_hbm, counts_hbm, inten_hbm, m_hbm, mt_hbm,
    grad_ref, mode_ref,
    object_ref, modes_ref, coeffs_ref, offsets_ref, region_ref, counts_ref, inten, m_ref, mt_ref,
    ext, nxt, mixes, stack, kron, kron_t, share, probes, windows,
    help_own, help_nxt, help_stack, help_share, carried, carried_out,
    terms, got_terms, acc, out_cols, got_cols, out_rows, got_rows, sums, out_sums, got_sums,
    local_sem, pair_send, pair_recv, mix_send, mix_recv, probe_send, probe_recv, term_send, term_recv,
):
    rows, cols, slots, num_modes, strip = dims
    size = cols * strip
    half = size // 2
    full = 2 * size
    split = num_modes * strip
    width = 2 * split
    r, c = lax.axis_index("row"), lax.axis_index("col")
    north, south = lax.rem(r + rows - 1, rows), lax.rem(r + 1, rows)
    west, east = lax.rem(c + cols - 1, cols), lax.rem(c + 1, cols)
    inner = pl.ds(half, size)
    low, high = pl.ds(half, half), pl.ds(size, half)
    first, last = pl.ds(0, half), pl.ds(size + half, half)
    others = pl.ds(0, cols - 1)
    side = cols // 4
    block = cols // 2
    plane, spot = lax.div(c, side), lax.rem(c, side)
    group = lax.div(c, block)
    outer = (plane == 0) | (plane == 3)
    helper = (plane == 1) | (plane == 2)
    across = lax.rem(c + block, cols)
    even = lax.rem(r, 2) == 0
    has_west, has_east = c > 0, c < cols - 1
    turn_west = (spot == 0) & has_west
    turn_east = (spot == side - 1) & has_east
    carry_west = (spot == side - 1) & (plane > 0)
    carry_east = (spot == 0) & (plane < 3)

    def remote(src, dst, index, device, sender=None):
        return pltpu.make_async_remote_copy(
            src_ref=src, dst_ref=dst,
            send_sem=pair_send.at[index if sender is None else sender], recv_sem=pair_recv.at[index],
            device_id=device, device_id_type=MESH,
        )

    def when(condition, *actions):
        @pl.when(condition)
        def _():
            for action in actions:
                action()

    def scatter(src, dst, send_sem, recv_sem, peer):
        return pltpu.make_async_remote_copy(
            src_ref=src, dst_ref=dst, send_sem=send_sem, recv_sem=recv_sem,
            device_id={"col": peer}, device_id_type=MESH,
        )

    def everyone(body):
        def step(k, carry):
            body(lax.rem(c + k, cols))
            return carry

        lax.fori_loop(1, cols, step, 0)

    def half_of(index, start, body):
        def step(k, carry):
            body(index * block + lax.rem(c + k, block))
            return carry

        lax.fori_loop(start, block, step, 0)

    def arrived(buffer, sem):
        pltpu.make_async_copy(buffer, buffer, sem).wait()

    barrier = pltpu.get_barrier_semaphore()
    everyone(lambda peer: pl.semaphore_signal(barrier, inc=1, device_id={"col": peer}, device_id_type=MESH))
    for peer in (north, south):
        pl.semaphore_signal(barrier, inc=1, device_id={"row": peer}, device_id_type=MESH)

    pl.semaphore_signal(barrier, inc=1, device_id={"row": south, "col": across}, device_id_type=MESH)
    pairs = [
        (coeffs_hbm, coeffs_ref), (region_hbm, region_ref), (modes_hbm, modes_ref), (object_hbm, object_ref),
        (offsets_hbm, offsets_ref), (counts_hbm, counts_ref), (inten_hbm, inten), (m_hbm, m_ref), (mt_hbm, mt_ref),
    ]
    loads = [pltpu.make_async_copy(src, dst, local_sem.at[i]) for i, (src, dst) in enumerate(pairs)]
    for load in loads:
        load.start()
    for load in loads[:2]:
        load.wait()
    mixes[c] = jnp.zeros((SLOT_ROWS, PAD), F32)
    for p in range(slots):
        weights = coeffs_ref[0, 0, p : p + 1, :]
        area = region_ref[0, :, p : p + 1]
        mixes[c, p : p + 1, :num_modes] = jnp.where(area == r, weights, 0.0)
        mixes[c, p : p + 1, num_modes : 2 * num_modes] = jnp.where(area == r + 1, weights, 0.0)
    for load in loads[2:4]:
        load.wait()
    ext[:, inner, inner] = object_ref[...].astype(BF16)
    pl.semaphore_wait(barrier, cols + 2)

    everyone(lambda peer: scatter(mixes.at[c], mixes.at[c], mix_send, mix_recv, peer).start())
    send_modes = remote(modes_ref, nxt, 0, {"row": north})
    help_modes = remote(modes_ref, help_own, 14, {"row": r, "col": across})
    help_next = remote(modes_ref, help_nxt, 15, {"row": north, "col": across})
    help_pass = remote(help_own, help_nxt, 15, {"row": north})
    when(outer, help_modes.start)
    send_modes.start()
    when(outer & even, help_next.start)
    to_north = remote(ext.at[:, low, inner], ext.at[:, last, inner], 1, {"row": north})
    to_south = remote(ext.at[:, high, inner], ext.at[:, first, inner], 2, {"row": south})
    to_west = remote(ext.at[:, inner, low], ext.at[:, inner, last], 3, {"col": west})
    to_east = remote(ext.at[:, inner, high], ext.at[:, inner, first], 4, {"col": east})
    west_turn = remote(ext.at[:, inner, low], carried.at[0], 16, {"col": c + side - 1})
    east_turn = remote(ext.at[:, inner, high], carried.at[1], 17, {"col": c - side + 1})
    west_pass = remote(carried.at[0], ext.at[:, inner, last], 3, {"col": c - side}, 18)
    east_pass = remote(carried.at[1], ext.at[:, inner, first], 4, {"col": c + side}, 19)
    go_west, go_east = has_west & (spot > 0), has_east & (spot < side - 1)
    when(turn_west, west_turn.start)
    when(turn_east, east_turn.start)
    to_north.start()
    to_south.start()
    when(go_west, to_west.start)
    when(go_east, to_east.start)

    def stack_modes(stack, modes, start):
        for part in range(2):
            stack[start : start + split, pl.ds(part * size, size)] = modes[0, :, part].reshape(split, size)

    stack_modes(stack, modes_ref, 0)
    stack[split:] = jnp.zeros((split, full), BF16)
    help_stack[split:] = jnp.zeros((split, full), BF16)

    arrived(mixes.at[others], mix_recv)
    mixed = mixes[...].reshape(cols * SLOT_ROWS, PAD)
    coarse = mixed.astype(BF16)
    fine = (mixed - coarse.astype(F32)).astype(BF16)
    repeat = where_bf16(iota((PAD, width), 0) == lax.div(iota((PAD, width), 1), strip))
    diagonal = iota((strip, width), 0) == lax.rem(iota((strip, width), 1), strip)
    for i, part in enumerate((coarse, fine)):
        wide = dot(part, repeat).reshape(cols, SLOT_ROWS, width)
        for p in range(slots):
            spread = jnp.where(diagonal[None], wide[:, p : p + 1, :], 0.0)
            kron[i, p] = spread.reshape(size, width).astype(BF16)

    def probe_copy(share, p, index, strip_index, peer):
        return scatter(share.at[p, index], probes.at[p, strip_index], probe_send.at[p], probe_recv.at[p], peer)

    def mix_slot(p):
        both = dot(kron[0, p], stack[...]) + dot(kron[1, p], stack[...])
        for part in range(2):
            value = both[:, part * size : (part + 1) * size].astype(BF16)
            share[p, :, part] = value.reshape(cols, strip, size)
        half_of(group, 1, lambda peer: probe_copy(share, p, peer, c, peer).start())
        when(helper, lambda: half_of(1 - group, 0, lambda peer: probe_copy(share, p, peer, c, peer).start()))
        probes[p, c] = share[p, c]

    def help_slot(p):
        @pl.when(helper)
        def _():
            lines = pl.ds(pl.multiple_of(group * half, half), half)
            both = dot(kron[0, p, lines], help_stack[...]) + dot(kron[1, p, lines], help_stack[...])
            for part in range(2):
                value = both[:, part * size : (part + 1) * size].astype(BF16)
                help_share[p, :, part] = value.reshape(block, strip, size)
            half_of(group, 1, lambda peer: probe_copy(help_share, p, lax.rem(peer, block), across, peer).start())
            probes[p, across] = help_share[p, lax.rem(c, block)]

    mix_slot(0)

    @pl.when(helper)
    def _():
        help_modes.wait_recv()
        when(jnp.logical_not(even), help_pass.start)
        stack_modes(help_stack, help_own, 0)

    help_slot(0)
    when(carry_west, west_turn.wait_recv, west_pass.start)
    when(carry_east, east_turn.wait_recv, east_pass.start)
    to_south.wait_recv()
    north_west = remote(ext.at[:, first, low], ext.at[:, first, last], 5, {"col": west})
    north_east = remote(ext.at[:, first, high], ext.at[:, first, first], 6, {"col": east})
    when(has_west, north_west.start)
    when(has_east, north_east.start)
    to_north.wait_recv()
    south_west = remote(ext.at[:, last, low], ext.at[:, last, last], 7, {"col": west})
    south_east = remote(ext.at[:, last, high], ext.at[:, last, first], 8, {"col": east})
    when(has_west, south_west.start)
    when(has_east, south_east.start)
    send_modes.wait_recv()
    stack_modes(stack, nxt, split)
    mix_slot(1)

    @pl.when(helper)
    def _():
        help_next.wait_recv()
        stack_modes(help_stack, help_nxt, split)

    help_slot(1)
    for p in range(2, slots):
        mix_slot(p)
        help_slot(p)

    repeat_t = where_bf16(iota((width, PAD), 1) == lax.div(iota((width, PAD), 0), strip))
    diagonal_t = lax.rem(iota((width, size), 0), strip) == lax.rem(iota((width, size), 1), strip)
    for i, part in enumerate((coarse, fine)):
        wide_t = lax.dot_general(repeat_t, part, (((1,), (1,)), ((), ())), preferred_element_type=F32).astype(BF16)
        for p in range(slots):
            sel_shape = (cols * SLOT_ROWS, size)
            select = where_bf16(iota(sel_shape, 0) == lax.div(iota(sel_shape, 1), strip) * SLOT_ROWS + p)
            kron_t[i, p] = jnp.where(diagonal_t, dot(wide_t, select), 0.0).astype(BF16)
    acc[...] = jnp.zeros_like(acc)
    for load in loads[4:]:
        load.wait()

    when(has_east, *(copy.wait_recv for copy in (to_west, north_west, south_west)))
    when(has_west, *(copy.wait_recv for copy in (to_east, north_east, south_east)))
    for copy in (to_north, to_south):
        copy.wait_send()
    when(go_west, to_west.wait_send)
    when(go_east, to_east.wait_send)
    when(turn_west, west_turn.wait_send)
    when(turn_east, east_turn.wait_send)
    when(has_west, north_west.wait_send, south_west.wait_send)
    when(has_east, north_east.wait_send, south_east.wait_send)
    for edge, box in (
        (r == 0, (slice(None), first, slice(None))),
        (r == rows - 1, (slice(None), last, slice(None))),
        (c == 0, (slice(None), pl.ds(0, full), first)),
        (c == cols - 1, (slice(None), pl.ds(0, full), last)),
    ):

        @pl.when(edge)
        def _(box=box):
            ext[box] = jnp.zeros_like(ext[box])

    def corner(p, axis):
        return offsets_ref[0, 0, axis : axis + 1, p : p + 1] + half

    for p in range(slots):
        pick_rows = where_bf16(iota((size, full), 1) == iota((size, full), 0) + corner(p, 0))
        pick_cols = where_bf16(iota((full, size), 0) == iota((full, size), 1) + corner(p, 1))
        for plane in range(2):
            narrow = dot(ext[plane], pick_cols).astype(BF16)
            windows[p, plane] = dot(pick_rows, narrow).astype(BF16)

    def send_terms(p):
        everyone(
            lambda peer: scatter(terms.at[p, peer], got_terms.at[p, c], term_send.at[p], term_recv.at[p], peer).start()
        )
        got_terms[p, c] = terms[p, c]

    def position(p):
        when(outer, lambda: arrived(probes.at[p, others], probe_recv.at[p]))
        when(helper, lambda: arrived(probes.at[p, pl.ds(0, cols - 2)], probe_recv.at[p]))
        pr_re = probes[p, :, 0].reshape(size, size).astype(F32)
        pr_im = probes[p, :, 1].reshape(size, size).astype(F32)
        w_re = windows[p, 0].astype(F32)
        w_im = windows[p, 1].astype(F32)
        e_re = (pr_re * w_re - pr_im * w_im).astype(BF16)
        e_im = (pr_re * w_im + pr_im * w_re).astype(BF16)
        left = dot(m_ref[...], jnp.concatenate([e_re, e_im], axis=0)).astype(BF16)
        far = dot(jnp.concatenate([left[:size], left[size:]], axis=1), mt_ref[...])
        f_re, f_im = far[:, :size], far[:, size:]
        energy = jnp.maximum(f_re * f_re + f_im * f_im, FLOOR * FLOOR)
        live = jnp.where(counts_ref[...] > p, 1.0, 0.0)
        factor = (jnp.sqrt(inten[0, 0, p].astype(F32)) * lax.rsqrt(energy) - 1.0) * live
        c_re = (f_re * factor).astype(BF16)
        c_im = (f_im * factor).astype(BF16)
        back = dot(mt_ref[...], jnp.concatenate([c_re, c_im], axis=0)).astype(BF16)
        update = dot(jnp.concatenate([back[:size], back[size:]], axis=1), m_ref[...])
        u_re, u_im = update[:, :size], update[:, size:]
        terms[p, :, 0] = (w_re * u_re + w_im * u_im).astype(BF16).reshape(cols, strip, size)
        terms[p, :, 1] = (w_re * u_im - w_im * u_re).astype(BF16).reshape(cols, strip, size)
        if p < slots - 1:
            send_terms(p)
        put_rows = where_bf16(iota((full, size), 0) == iota((full, size), 1) + corner(p, 0))
        put_cols = where_bf16(iota((size, full), 1) == iota((size, full), 0) + corner(p, 1))
        for plane, value in enumerate((pr_re * u_re + pr_im * u_im, pr_re * u_im - pr_im * u_re)):
            acc[plane] += dot(put_rows, dot(value.astype(BF16), put_cols).astype(BF16))

    for p in range(slots):
        position(p)

    out_cols[0] = acc[:, :, first].astype(BF16)
    out_cols[1] = acc[:, :, last].astype(BF16)
    top, bottom = pl.ds(0, size), pl.ds(size, size)
    cols_west = [remote(out_cols.at[0, :, rows_of], got_cols.at[1, :, rows_of], i, {"col": west})
                 for i, rows_of in ((9, top), (20, bottom))]
    cols_east = [remote(out_cols.at[1, :, rows_of], got_cols.at[0, :, rows_of], i, {"col": east})
                 for i, rows_of in ((10, top), (21, bottom))]
    west_turn_out = remote(out_cols.at[0, :, top], carried_out.at[0], 22, {"col": c + side - 1})
    east_turn_out = remote(out_cols.at[1, :, top], carried_out.at[1], 23, {"col": c - side + 1})
    west_pass_out = remote(carried_out.at[0], got_cols.at[1, :, top], 9, {"col": c - side}, 24)
    east_pass_out = remote(carried_out.at[1], got_cols.at[0, :, top], 10, {"col": c + side}, 25)
    when(turn_west, west_turn_out.start)
    when(turn_east, east_turn_out.start)
    when(go_west, cols_west[0].start)
    when(go_east, cols_east[0].start)
    when(has_west, cols_west[1].start)
    when(has_east, cols_east[1].start)
    send_terms(slots - 1)

    def gather(p, part_of):
        both = jnp.concatenate([got_terms[p, :, plane].reshape(size, size) for plane in range(2)], axis=1)
        where = pl.ds(part_of * split, split)
        value = dot(kron_t[0, p, where], both) + dot(kron_t[1, p, where], both)
        if p == 0:
            sums[where] = value
        else:
            sums[where] += value

    arrived(got_terms.at[0, others], term_recv.at[0])
    gather(0, 1)
    when(carry_west, west_turn_out.wait_recv, west_pass_out.start)
    when(carry_east, east_turn_out.wait_recv, east_pass_out.start)
    for p in range(1, slots - 2):
        arrived(got_terms.at[p, others], term_recv.at[p])
        gather(p, 1)

    when(has_west, *(copy.wait_recv for copy in cols_east))
    acc[:, :, low] += jnp.where(c == 0, 0.0, got_cols[0].astype(F32))
    when(has_east, *(copy.wait_recv for copy in cols_west))
    acc[:, :, high] += jnp.where(c == cols - 1, 0.0, got_cols[1].astype(F32))
    out_rows[0] = acc[:, first, inner].astype(BF16)
    out_rows[1] = acc[:, last, inner].astype(BF16)
    rows_north = remote(out_rows.at[0], got_rows.at[1], 11, {"row": north})
    rows_south = remote(out_rows.at[1], got_rows.at[0], 12, {"row": south})
    rows_north.start()
    rows_south.start()

    for p in range(slots - 2, slots):
        arrived(got_terms.at[p, others], term_recv.at[p])
        gather(p, 1)
    for plane in range(2):
        part = sums[split:, pl.ds(plane * size, size)].astype(BF16)
        out_sums[:, plane] = part.reshape(num_modes, strip, size)
    send_sums = remote(out_sums, got_sums, 13, {"row": south})
    send_sums.start()
    for p in range(slots):
        gather(p, 0)

    rows_south.wait_recv()
    grad_ref[:, pl.ds(0, half), :] = acc[:, low, inner] + jnp.where(r == 0, 0.0, got_rows[0].astype(F32))
    rows_north.wait_recv()
    grad_ref[:, pl.ds(half, half), :] = acc[:, high, inner] + jnp.where(r == rows - 1, 0.0, got_rows[1].astype(F32))
    send_sums.wait_recv()
    for plane in range(2):
        own = sums[:split, pl.ds(plane * size, size)].reshape(num_modes, strip, size)
        mode_ref[0, :, plane] = own + got_sums[:, plane].astype(F32)

    for copy in (send_modes, rows_north, rows_south, send_sums):
        copy.wait_send()
    when(outer, help_modes.wait_send)
    when(outer & even, help_next.wait_send)
    when(helper & jnp.logical_not(even), help_pass.wait_send)
    when(carry_west, west_pass.wait_send, west_pass_out.wait_send)
    when(carry_east, east_pass.wait_send, east_pass_out.wait_send)
    when(turn_west, west_turn_out.wait_send)
    when(turn_east, east_turn_out.wait_send)
    when(go_west, cols_west[0].wait_send)
    when(go_east, cols_east[0].wait_send)
    when(has_west, cols_west[1].wait_send)
    when(has_east, cols_east[1].wait_send)
    arrived(mixes.at[others], mix_send)
    for p in range(slots):
        near = pl.ds(0, block - 1)
        arrived(share.at[p, near], probe_send.at[p])
        when(helper, lambda p=p: arrived(share.at[p, pl.ds(0, block)], probe_send.at[p]))
        when(helper, lambda p=p: arrived(help_share.at[p, near], probe_send.at[p]))
        arrived(terms.at[p, others], term_send.at[p])


def local(object_field, modes, coeffs, offsets, region, counts, intensity):
    size = modes.shape[-1]
    half = size // 2
    full = 2 * size
    num_modes = modes.shape[1]
    slots = coeffs.shape[2]
    strip = modes.shape[3]
    rows, cols = lax.axis_size("row"), lax.axis_size("col")
    block, block_t = dft_blocks(size)
    width = 2 * num_modes * strip
    vmem = pl.BlockSpec(memory_space=pltpu.VMEM)
    hbm = pl.BlockSpec(memory_space=pl.ANY)
    pieces = (slots, cols, 2, strip, size)
    dma = pltpu.SemaphoreType.DMA
    args = (
        object_field, modes, coeffs, jnp.swapaxes(offsets, 2, 3), region, counts, intensity, jnp.asarray(block), jnp.asarray(block_t),
    )
    return pl.pallas_call(
        functools.partial(kernel, (rows, cols, slots, num_modes, strip)),
        out_shape=(
            pltpu.VMEM((2, size, size), F32),
            pltpu.VMEM((1, num_modes, 2, strip, size), F32),
        ),
        in_specs=[hbm] * len(args),
        out_specs=(vmem, vmem),
        scratch_shapes=[pltpu.VMEM(x.shape, x.dtype) for x in args]
        + [
            pltpu.VMEM((2, full, full), BF16),
            pltpu.VMEM(modes.shape, BF16),
            pltpu.VMEM((cols, SLOT_ROWS, PAD), F32),
            pltpu.VMEM((width, full), BF16),
            pltpu.VMEM((2, slots, size, width), BF16),
            pltpu.VMEM((2, slots, width, size), BF16),
            pltpu.VMEM(pieces, BF16),
            pltpu.VMEM(pieces, BF16),
            pltpu.VMEM((slots, 2, size, size), BF16),
            pltpu.VMEM(modes.shape, BF16),
            pltpu.VMEM(modes.shape, BF16),
            pltpu.VMEM((width, full), BF16),
            pltpu.VMEM((slots, cols // 2, 2, strip, size), BF16),
            pltpu.VMEM((2, 2, size, half), BF16),
            pltpu.VMEM((2, 2, size, half), BF16),
            pltpu.VMEM(pieces, BF16),
            pltpu.VMEM(pieces, BF16),
            pltpu.VMEM((2, full, full), F32),
            pltpu.VMEM((2, 2, full, half), BF16),
            pltpu.VMEM((2, 2, full, half), BF16),
            pltpu.VMEM((2, 2, half, size), BF16),
            pltpu.VMEM((2, 2, half, size), BF16),
            pltpu.VMEM((width, full), F32),
            pltpu.VMEM((num_modes, 2, strip, size), BF16),
            pltpu.VMEM((num_modes, 2, strip, size), BF16),
            dma((len(args),)),
            dma((26,)),
            dma((26,)),
            dma,
            dma,
            dma((slots,)),
            dma((slots,)),
            dma((slots,)),
            dma((slots,)),
        ],
        compiler_params=pltpu.CompilerParams(
            collective_id=0, has_side_effects=True, vmem_limit_bytes=56 << 20
        ),
        name="ptychography",
    )(*args)


def solution(mesh):
    in_specs = (
        P(None, "row", "col"),
        P("row", None, None, "col", None),
        P("row", "col", None, None),
        P("row", "col", None, None),
        P("row", "col", None),
        P("row", "col"),
        P("row", "col", None, None, None),
    )
    out_specs = (P(None, "row", "col"), P("row", None, None, "col", None))
    return jax.shard_map(local, mesh=mesh, in_specs=in_specs, out_specs=out_specs, check_vma=False)
```

```python
import functools
import math

import jax
import jax.numpy as jnp
import numpy as np
from jax import lax
from jax.experimental import pallas as pl
from jax.experimental.pallas import tpu as pltpu
from jax.sharding import PartitionSpec as P

FLOOR = 0.25
PAD = 128
SLOT_ROWS = 8
F32 = jnp.float32
BF16 = jnp.bfloat16
MESH = pl.DeviceIdType.MESH


def dft_blocks(length):
    index = np.arange(length)
    angles = (index[:, None] * index[None, :] % length).astype(np.float32) * np.float32(2.0 * math.pi / length)
    scaling = np.float32(1.0 / math.sqrt(length))
    re = (np.cos(angles) * scaling).astype(jnp.bfloat16)
    im = (-np.sin(angles) * scaling).astype(jnp.bfloat16)
    block = np.block([[re, -im], [im, re]])
    return block, np.ascontiguousarray(block.T)


def dot(a, b):
    return jnp.dot(a, b, preferred_element_type=F32)


def iota(shape, dim):
    return lax.broadcasted_iota(jnp.int32, shape, dim)


def where_bf16(mask):
    return jnp.where(mask, 1.0, 0.0).astype(BF16)


def kernel(
    dims,
    object_hbm, modes_hbm, coeffs_hbm, offsets_hbm, region_hbm, counts_hbm, inten_hbm, m_hbm, mt_hbm,
    grad_ref, mode_ref,
    object_ref, modes_ref, coeffs_ref, offsets_ref, region_ref, counts_ref, inten, m_ref, mt_ref,
    ext, nxt, mixes, stack, kron, kron_t, share, probes, windows,
    help_own, help_nxt, help_stack, help_share, carried, carried_out,
    terms, got_terms, acc, out_cols, got_cols, out_rows, got_rows, sums, out_sums, got_sums,
    local_sem, pair_send, pair_recv, mix_send, mix_recv, probe_send, probe_recv, term_send, term_recv,
):
    rows, cols, slots, num_modes, strip = dims
    size = cols * strip
    half = size // 2
    full = 2 * size
    split = num_modes * strip
    width = 2 * split
    r, c = lax.axis_index("row"), lax.axis_index("col")
    north, south = lax.rem(r + rows - 1, rows), lax.rem(r + 1, rows)
    west, east = lax.rem(c + cols - 1, cols), lax.rem(c + 1, cols)
    inner = pl.ds(half, size)
    low, high = pl.ds(half, half), pl.ds(size, half)
    first, last = pl.ds(0, half), pl.ds(size + half, half)
    others = pl.ds(0, cols - 1)
    side = cols // 4
    block = cols // 2
    plane, spot = lax.div(c, side), lax.rem(c, side)
    group = lax.div(c, block)
    outer = (plane == 0) | (plane == 3)
    helper = (plane == 1) | (plane == 2)
    across = lax.rem(c + block, cols)
    even = lax.rem(r, 2) == 0
    has_west, has_east = c > 0, c < cols - 1
    turn_west = (spot == 0) & has_west
    turn_east = (spot == side - 1) & has_east
    carry_west = (spot == side - 1) & (plane > 0)
    carry_east = (spot == 0) & (plane < 3)
    pass_west = (spot > 0) & (plane > 0)
    pass_east = (spot < side - 1) & (plane < 3)
    west_end, east_end = plane * side - 1, (plane + 1) * side

    def remote(src, dst, index, device, sender=None):
        return pltpu.make_async_remote_copy(
            src_ref=src, dst_ref=dst,
            send_sem=pair_send.at[index if sender is None else sender], recv_sem=pair_recv.at[index],
            device_id=device, device_id_type=MESH,
        )

    def when(condition, *actions):
        @pl.when(condition)
        def _():
            for action in actions:
                action()

    def scatter(src, dst, send_sem, recv_sem, peer):
        return pltpu.make_async_remote_copy(
            src_ref=src, dst_ref=dst, send_sem=send_sem, recv_sem=recv_sem,
            device_id={"col": peer}, device_id_type=MESH,
        )

    def everyone(body):
        def step(k, carry):
            body(lax.rem(c + k, cols))
            return carry

        lax.fori_loop(1, cols, step, 0)

    def half_of(index, start, body):
        def step(k, carry):
            body(index * block + lax.rem(c + k, block))
            return carry

        lax.fori_loop(start, block, step, 0)

    def arrived(buffer, sem):
        pltpu.make_async_copy(buffer, buffer, sem).wait()

    barrier = pltpu.get_barrier_semaphore()
    everyone(lambda peer: pl.semaphore_signal(barrier, inc=1, device_id={"col": peer}, device_id_type=MESH))
    for peer in (north, south):
        pl.semaphore_signal(barrier, inc=1, device_id={"row": peer}, device_id_type=MESH)

    pl.semaphore_signal(barrier, inc=1, device_id={"row": south, "col": across}, device_id_type=MESH)
    pairs = [
        (coeffs_hbm, coeffs_ref), (region_hbm, region_ref), (modes_hbm, modes_ref), (object_hbm, object_ref),
        (offsets_hbm, offsets_ref), (counts_hbm, counts_ref), (inten_hbm, inten), (m_hbm, m_ref), (mt_hbm, mt_ref),
    ]
    loads = [pltpu.make_async_copy(src, dst, local_sem.at[i]) for i, (src, dst) in enumerate(pairs)]
    for load in loads:
        load.start()
    for load in loads[:2]:
        load.wait()
    mixes[c] = jnp.zeros((SLOT_ROWS, PAD), F32)
    for p in range(slots):
        weights = coeffs_ref[0, 0, p : p + 1, :]
        area = region_ref[0, :, p : p + 1]
        mixes[c, p : p + 1, :num_modes] = jnp.where(area == r, weights, 0.0)
        mixes[c, p : p + 1, num_modes : 2 * num_modes] = jnp.where(area == r + 1, weights, 0.0)
    for load in loads[2:4]:
        load.wait()
    ext[:, inner, inner] = object_ref[...].astype(BF16)
    pl.semaphore_wait(barrier, cols + 2)

    everyone(lambda peer: scatter(mixes.at[c], mixes.at[c], mix_send, mix_recv, peer).start())
    send_modes = remote(modes_ref, nxt, 0, {"row": north})
    help_modes = remote(modes_ref, help_own, 14, {"row": r, "col": across})
    help_next = remote(modes_ref, help_nxt, 15, {"row": north, "col": across})
    help_pass = remote(help_own, help_nxt, 15, {"row": north})
    when(outer, help_modes.start)
    send_modes.start()
    when(outer & even, help_next.start)
    to_north = remote(ext.at[:, low, inner], ext.at[:, last, inner], 1, {"row": north})
    to_south = remote(ext.at[:, high, inner], ext.at[:, first, inner], 2, {"row": south})
    to_west = remote(ext.at[:, inner, low], ext.at[:, inner, last], 3, {"col": west})
    to_east = remote(ext.at[:, inner, high], ext.at[:, inner, first], 4, {"col": east})
    west_turn = remote(ext.at[:, inner, low], carried.at[0], 16, {"col": c + side - 1})
    east_turn = remote(ext.at[:, inner, high], carried.at[1], 17, {"col": c - side + 1})
    west_pass = remote(carried.at[0], ext.at[:, inner, last], 3, {"col": c - side}, 18)
    east_pass = remote(carried.at[1], ext.at[:, inner, first], 4, {"col": c + side}, 19)
    go_west, go_east = has_west & (spot > 0), has_east & (spot < side - 1)
    when(turn_west, west_turn.start)
    when(turn_east, east_turn.start)
    to_north.start()
    to_south.start()
    when(go_west, to_west.start)
    when(go_east, to_east.start)

    def stack_modes(stack, modes, start):
        for part in range(2):
            stack[start : start + split, pl.ds(part * size, size)] = modes[0, :, part].reshape(split, size)

    stack_modes(stack, modes_ref, 0)
    stack[split:] = jnp.zeros((split, full), BF16)
    help_stack[split:] = jnp.zeros((split, full), BF16)

    arrived(mixes.at[others], mix_recv)
    mixed = mixes[...].reshape(cols * SLOT_ROWS, PAD)
    coarse = mixed.astype(BF16)
    fine = (mixed - coarse.astype(F32)).astype(BF16)
    repeat = where_bf16(iota((PAD, width), 0) == lax.div(iota((PAD, width), 1), strip))
    diagonal = iota((strip, width), 0) == lax.rem(iota((strip, width), 1), strip)
    for i, part in enumerate((coarse, fine)):
        wide = dot(part, repeat).reshape(cols, SLOT_ROWS, width)
        for p in range(slots):
            spread = jnp.where(diagonal[None], wide[:, p : p + 1, :], 0.0)
            kron[i, p] = spread.reshape(size, width).astype(BF16)

    def probe_copy(share, p, index, strip_index, peer):
        return scatter(share.at[p, index], probes.at[p, strip_index], probe_send.at[p], probe_recv.at[p], peer)

    def mix_slot(p):
        both = dot(kron[0, p], stack[...]) + dot(kron[1, p], stack[...])
        for part in range(2):
            value = both[:, part * size : (part + 1) * size].astype(BF16)
            share[p, :, part] = value.reshape(cols, strip, size)
        half_of(group, 1, lambda peer: probe_copy(share, p, peer, c, peer).start())
        when(helper, lambda: half_of(1 - group, 0, lambda peer: probe_copy(share, p, peer, c, peer).start()))
        probes[p, c] = share[p, c]

    def help_slot(p):
        @pl.when(helper)
        def _():
            lines = pl.ds(pl.multiple_of(group * half, half), half)
            both = dot(kron[0, p, lines], help_stack[...]) + dot(kron[1, p, lines], help_stack[...])
            for part in range(2):
                value = both[:, part * size : (part + 1) * size].astype(BF16)
                help_share[p, :, part] = value.reshape(block, strip, size)
            half_of(group, 1, lambda peer: probe_copy(help_share, p, lax.rem(peer, block), across, peer).start())
            probes[p, across] = help_share[p, lax.rem(c, block)]

    mix_slot(0)

    @pl.when(helper)
    def _():
        help_modes.wait_recv()
        when(jnp.logical_not(even), help_pass.start)
        stack_modes(help_stack, help_own, 0)

    help_slot(0)
    when(carry_west, west_turn.wait_recv, west_pass.start)
    when(carry_east, east_turn.wait_recv, east_pass.start)
    to_south.wait_recv()
    north_west = remote(ext.at[:, first, low], ext.at[:, first, last], 5, {"col": west})
    north_east = remote(ext.at[:, first, high], ext.at[:, first, first], 6, {"col": east})
    when(has_west, north_west.start)
    when(has_east, north_east.start)
    to_north.wait_recv()
    south_west = remote(ext.at[:, last, low], ext.at[:, last, last], 7, {"col": west})
    south_east = remote(ext.at[:, last, high], ext.at[:, last, first], 8, {"col": east})
    when(has_west, south_west.start)
    when(has_east, south_east.start)
    send_modes.wait_recv()
    stack_modes(stack, nxt, split)
    mix_slot(1)

    @pl.when(helper)
    def _():
        help_next.wait_recv()
        stack_modes(help_stack, help_nxt, split)

    help_slot(1)
    for p in range(2, slots):
        mix_slot(p)
        help_slot(p)

    repeat_t = where_bf16(iota((width, PAD), 1) == lax.div(iota((width, PAD), 0), strip))
    diagonal_t = lax.rem(iota((width, size), 0), strip) == lax.rem(iota((width, size), 1), strip)
    for i, part in enumerate((coarse, fine)):
        wide_t = lax.dot_general(repeat_t, part, (((1,), (1,)), ((), ())), preferred_element_type=F32).astype(BF16)
        for p in range(slots):
            sel_shape = (cols * SLOT_ROWS, size)
            select = where_bf16(iota(sel_shape, 0) == lax.div(iota(sel_shape, 1), strip) * SLOT_ROWS + p)
            kron_t[i, p] = jnp.where(diagonal_t, dot(wide_t, select), 0.0).astype(BF16)
    acc[...] = jnp.zeros_like(acc)
    for load in loads[4:]:
        load.wait()

    when(has_east, *(copy.wait_recv for copy in (to_west, north_west, south_west)))
    when(has_west, *(copy.wait_recv for copy in (to_east, north_east, south_east)))
    for copy in (to_north, to_south):
        copy.wait_send()
    when(go_west, to_west.wait_send)
    when(go_east, to_east.wait_send)
    when(turn_west, west_turn.wait_send)
    when(turn_east, east_turn.wait_send)
    when(has_west, north_west.wait_send, south_west.wait_send)
    when(has_east, north_east.wait_send, south_east.wait_send)
    for edge, box in (
        (r == 0, (slice(None), first, slice(None))),
        (r == rows - 1, (slice(None), last, slice(None))),
        (c == 0, (slice(None), pl.ds(0, full), first)),
        (c == cols - 1, (slice(None), pl.ds(0, full), last)),
    ):

        @pl.when(edge)
        def _(box=box):
            ext[box] = jnp.zeros_like(ext[box])

    def corner(p, axis):
        return offsets_ref[0, 0, axis : axis + 1, p : p + 1] + half

    for p in range(slots):
        pick_rows = where_bf16(iota((size, full), 1) == iota((size, full), 0) + corner(p, 0))
        pick_cols = where_bf16(iota((full, size), 0) == iota((full, size), 1) + corner(p, 1))
        for plane in range(2):
            narrow = dot(ext[plane], pick_cols).astype(BF16)
            windows[p, plane] = dot(pick_rows, narrow).astype(BF16)

    def send_terms(p):
        everyone(
            lambda peer: scatter(terms.at[p, peer], got_terms.at[p, c], term_send.at[p], term_recv.at[p], peer).start()
        )
        got_terms[p, c] = terms[p, c]

    def position(p):
        when(outer, lambda: arrived(probes.at[p, others], probe_recv.at[p]))
        when(helper, lambda: arrived(probes.at[p, pl.ds(0, cols - 2)], probe_recv.at[p]))
        pr_re = probes[p, :, 0].reshape(size, size).astype(F32)
        pr_im = probes[p, :, 1].reshape(size, size).astype(F32)
        w_re = windows[p, 0].astype(F32)
        w_im = windows[p, 1].astype(F32)
        e_re = (pr_re * w_re - pr_im * w_im).astype(BF16)
        e_im = (pr_re * w_im + pr_im * w_re).astype(BF16)
        left = dot(m_ref[...], jnp.concatenate([e_re, e_im], axis=0)).astype(BF16)
        far = dot(jnp.concatenate([left[:size], left[size:]], axis=1), mt_ref[...])
        f_re, f_im = far[:, :size], far[:, size:]
        energy = jnp.maximum(f_re * f_re + f_im * f_im, FLOOR * FLOOR)
        live = jnp.where(counts_ref[...] > p, 1.0, 0.0)
        factor = (jnp.sqrt(inten[0, 0, p].astype(F32)) * lax.rsqrt(energy) - 1.0) * live
        c_re = (f_re * factor).astype(BF16)
        c_im = (f_im * factor).astype(BF16)
        back = dot(mt_ref[...], jnp.concatenate([c_re, c_im], axis=0)).astype(BF16)
        update = dot(jnp.concatenate([back[:size], back[size:]], axis=1), m_ref[...])
        u_re, u_im = update[:, :size], update[:, size:]
        terms[p, :, 0] = (w_re * u_re + w_im * u_im).astype(BF16).reshape(cols, strip, size)
        terms[p, :, 1] = (w_re * u_im - w_im * u_re).astype(BF16).reshape(cols, strip, size)
        if p < slots - 1:
            send_terms(p)
        put_rows = where_bf16(iota((full, size), 0) == iota((full, size), 1) + corner(p, 0))
        put_cols = where_bf16(iota((size, full), 1) == iota((size, full), 0) + corner(p, 1))
        for plane, value in enumerate((pr_re * u_re + pr_im * u_im, pr_re * u_im - pr_im * u_re)):
            acc[plane] += dot(put_rows, dot(value.astype(BF16), put_cols).astype(BF16))

    for p in range(slots):
        position(p)

    out_cols[0] = acc[:, :, first].astype(BF16)
    out_cols[1] = acc[:, :, last].astype(BF16)
    quarter = full // 4

    def piece(buffer, side_of, i):
        return buffer.at[side_of, :, pl.ds(pl.multiple_of(i * quarter, quarter), quarter)]

    cols_west = remote(out_cols.at[0], got_cols.at[1], 9, {"col": west})
    cols_east = remote(out_cols.at[1], got_cols.at[0], 10, {"col": east})
    west_parts = [remote(piece(out_cols, 0, i), piece(got_cols, 1, i), 26 + i, {"col": west}) for i in range(4)]
    east_parts = [remote(piece(out_cols, 1, i), piece(got_cols, 0, i), 30 + i, {"col": east}) for i in range(4)]
    west_turns = [remote(piece(out_cols, 0, i), carried_out.at[0], 22, {"col": c + i}, 34 + i) for i in range(1, 4)]
    east_turns = [remote(piece(out_cols, 1, i), carried_out.at[1], 23, {"col": c - 3 + i}, 38 + i) for i in range(3)]
    west_pass_out = remote(carried_out.at[0], piece(got_cols, 1, spot), 26 + spot, {"col": west_end}, 24)
    east_pass_out = remote(carried_out.at[1], piece(got_cols, 0, spot), 30 + spot, {"col": east_end}, 25)
    when(turn_west, *(copy.start for copy in west_turns), west_parts[0].start)
    when(turn_east, *(copy.start for copy in east_turns), east_parts[3].start)
    when(go_west, cols_west.start)
    when(go_east, cols_east.start)
    send_terms(slots - 1)

    def gather(p, part_of):
        both = jnp.concatenate([got_terms[p, :, plane].reshape(size, size) for plane in range(2)], axis=1)
        where = pl.ds(part_of * split, split)
        value = dot(kron_t[0, p, where], both) + dot(kron_t[1, p, where], both)
        if p == 0:
            sums[where] = value
        else:
            sums[where] += value

    arrived(got_terms.at[0, others], term_recv.at[0])
    gather(0, 1)
    when(pass_west, west_turns[0].wait_recv, west_pass_out.start)
    when(pass_east, east_turns[0].wait_recv, east_pass_out.start)
    for p in range(1, slots - 2):
        arrived(got_terms.at[p, others], term_recv.at[p])
        gather(p, 1)

    when(go_west, cols_east.wait_recv)
    when(turn_west, *(copy.wait_recv for copy in east_parts))
    acc[:, :, low] += jnp.where(c == 0, 0.0, got_cols[0].astype(F32))
    when(go_east, cols_west.wait_recv)
    when(turn_east, *(copy.wait_recv for copy in west_parts))
    acc[:, :, high] += jnp.where(c == cols - 1, 0.0, got_cols[1].astype(F32))
    out_rows[0] = acc[:, first, inner].astype(BF16)
    out_rows[1] = acc[:, last, inner].astype(BF16)
    rows_north = remote(out_rows.at[0], got_rows.at[1], 11, {"row": north})
    rows_south = remote(out_rows.at[1], got_rows.at[0], 12, {"row": south})
    rows_north.start()
    rows_south.start()

    for p in range(slots - 2, slots):
        arrived(got_terms.at[p, others], term_recv.at[p])
        gather(p, 1)
    for plane in range(2):
        part = sums[split:, pl.ds(plane * size, size)].astype(BF16)
        out_sums[:, plane] = part.reshape(num_modes, strip, size)
    send_sums = remote(out_sums, got_sums, 13, {"row": south})
    send_sums.start()
    for p in range(slots):
        gather(p, 0)

    rows_south.wait_recv()
    grad_ref[:, pl.ds(0, half), :] = acc[:, low, inner] + jnp.where(r == 0, 0.0, got_rows[0].astype(F32))
    rows_north.wait_recv()
    grad_ref[:, pl.ds(half, half), :] = acc[:, high, inner] + jnp.where(r == rows - 1, 0.0, got_rows[1].astype(F32))
    send_sums.wait_recv()
    for plane in range(2):
        own = sums[:split, pl.ds(plane * size, size)].reshape(num_modes, strip, size)
        mode_ref[0, :, plane] = own + got_sums[:, plane].astype(F32)

    for copy in (send_modes, rows_north, rows_south, send_sums):
        copy.wait_send()
    when(outer, help_modes.wait_send)
    when(outer & even, help_next.wait_send)
    when(helper & jnp.logical_not(even), help_pass.wait_send)
    when(carry_west, west_pass.wait_send)
    when(carry_east, east_pass.wait_send)
    when(pass_west, west_pass_out.wait_send)
    when(pass_east, east_pass_out.wait_send)
    when(turn_west, *(copy.wait_send for copy in west_turns), west_parts[0].wait_send)
    when(turn_east, *(copy.wait_send for copy in east_turns), east_parts[3].wait_send)
    when(go_west, cols_west.wait_send)
    when(go_east, cols_east.wait_send)
    arrived(mixes.at[others], mix_send)
    for p in range(slots):
        near = pl.ds(0, block - 1)
        arrived(share.at[p, near], probe_send.at[p])
        when(helper, lambda p=p: arrived(share.at[p, pl.ds(0, block)], probe_send.at[p]))
        when(helper, lambda p=p: arrived(help_share.at[p, near], probe_send.at[p]))
        arrived(terms.at[p, others], term_send.at[p])


def local(object_field, modes, coeffs, offsets, region, counts, intensity):
    size = modes.shape[-1]
    half = size // 2
    full = 2 * size
    num_modes = modes.shape[1]
    slots = coeffs.shape[2]
    strip = modes.shape[3]
    rows, cols = lax.axis_size("row"), lax.axis_size("col")
    block, block_t = dft_blocks(size)
    width = 2 * num_modes * strip
    vmem = pl.BlockSpec(memory_space=pltpu.VMEM)
    hbm = pl.BlockSpec(memory_space=pl.ANY)
    pieces = (slots, cols, 2, strip, size)
    dma = pltpu.SemaphoreType.DMA
    args = (
        object_field, modes, coeffs, jnp.swapaxes(offsets, 2, 3), region, counts, intensity, jnp.asarray(block), jnp.asarray(block_t),
    )
    return pl.pallas_call(
        functools.partial(kernel, (rows, cols, slots, num_modes, strip)),
        out_shape=(
            pltpu.VMEM((2, size, size), F32),
            pltpu.VMEM((1, num_modes, 2, strip, size), F32),
        ),
        in_specs=[hbm] * len(args),
        out_specs=(vmem, vmem),
        scratch_shapes=[pltpu.VMEM(x.shape, x.dtype) for x in args]
        + [
            pltpu.VMEM((2, full, full), BF16),
            pltpu.VMEM(modes.shape, BF16),
            pltpu.VMEM((cols, SLOT_ROWS, PAD), F32),
            pltpu.VMEM((width, full), BF16),
            pltpu.VMEM((2, slots, size, width), BF16),
            pltpu.VMEM((2, slots, width, size), BF16),
            pltpu.VMEM(pieces, BF16),
            pltpu.VMEM(pieces, BF16),
            pltpu.VMEM((slots, 2, size, size), BF16),
            pltpu.VMEM(modes.shape, BF16),
            pltpu.VMEM(modes.shape, BF16),
            pltpu.VMEM((width, full), BF16),
            pltpu.VMEM((slots, cols // 2, 2, strip, size), BF16),
            pltpu.VMEM((2, 2, size, half), BF16),
            pltpu.VMEM((2, 2, full // 4, half), BF16),
            pltpu.VMEM(pieces, BF16),
            pltpu.VMEM(pieces, BF16),
            pltpu.VMEM((2, full, full), F32),
            pltpu.VMEM((2, 2, full, half), BF16),
            pltpu.VMEM((2, 2, full, half), BF16),
            pltpu.VMEM((2, 2, half, size), BF16),
            pltpu.VMEM((2, 2, half, size), BF16),
            pltpu.VMEM((width, full), F32),
            pltpu.VMEM((num_modes, 2, strip, size), BF16),
            pltpu.VMEM((num_modes, 2, strip, size), BF16),
            dma((len(args),)),
            dma((42,)),
            dma((42,)),
            dma,
            dma,
            dma((slots,)),
            dma((slots,)),
            dma((slots,)),
            dma((slots,)),
        ],
        compiler_params=pltpu.CompilerParams(
            collective_id=0, has_side_effects=True, vmem_limit_bytes=56 << 20
        ),
        name="ptychography",
    )(*args)


def solution(mesh):
    in_specs = (
        P(None, "row", "col"),
        P("row", None, None, "col", None),
        P("row", "col", None, None),
        P("row", "col", None, None),
        P("row", "col", None),
        P("row", "col"),
        P("row", "col", None, None, None),
    )
    out_specs = (P(None, "row", "col"), P("row", None, None, "col", None))
    return jax.shard_map(local, mesh=mesh, in_specs=in_specs, out_specs=out_specs, check_vma=False)
```

```python
import functools
import math

import jax
import jax.numpy as jnp
import numpy as np
from jax import lax
from jax.experimental import pallas as pl
from jax.experimental.pallas import tpu as pltpu
from jax.sharding import PartitionSpec as P

FLOOR = 0.25
PAD = 128
SLOT_ROWS = 8
F32 = jnp.float32
BF16 = jnp.bfloat16
MESH = pl.DeviceIdType.MESH


def dft_blocks(length):
    index = np.arange(length)
    angles = (index[:, None] * index[None, :] % length).astype(np.float32) * np.float32(2.0 * math.pi / length)
    scaling = np.float32(1.0 / math.sqrt(length))
    re = (np.cos(angles) * scaling).astype(jnp.bfloat16)
    im = (-np.sin(angles) * scaling).astype(jnp.bfloat16)
    block = np.block([[re, -im], [im, re]])
    return block, np.ascontiguousarray(block.T)


def dot(a, b):
    return jnp.dot(a, b, preferred_element_type=F32)


def iota(shape, dim):
    return lax.broadcasted_iota(jnp.int32, shape, dim)


def where_bf16(mask):
    return jnp.where(mask, 1.0, 0.0).astype(BF16)


def kernel(
    dims,
    object_hbm, modes_hbm, coeffs_hbm, offsets_hbm, region_hbm, counts_hbm, inten_hbm, m_hbm, mt_hbm,
    grad_ref, mode_ref,
    object_ref, modes_ref, coeffs_ref, offsets_ref, region_ref, counts_ref, inten, m_ref, mt_ref,
    ext, nxt, mixes, stack, kron, kron_t, share, probes, windows,
    help_own, help_nxt, help_stack, help_share, carried, carried_out,
    terms, got_terms, acc, out_cols, got_cols, out_rows, got_rows, sums, out_sums, got_sums,
    local_sem, pair_send, pair_recv, mix_send, mix_recv, probe_send, probe_recv, term_send, term_recv,
):
    rows, cols, slots, num_modes, strip = dims
    size = cols * strip
    half = size // 2
    full = 2 * size
    split = num_modes * strip
    width = 2 * split
    r, c = lax.axis_index("row"), lax.axis_index("col")
    north, south = lax.rem(r + rows - 1, rows), lax.rem(r + 1, rows)
    west, east = lax.rem(c + cols - 1, cols), lax.rem(c + 1, cols)
    inner = pl.ds(half, size)
    low, high = pl.ds(half, half), pl.ds(size, half)
    first, last = pl.ds(0, half), pl.ds(size + half, half)
    others = pl.ds(0, cols - 1)
    side = cols // 4
    block = cols // 2
    plane, spot = lax.div(c, side), lax.rem(c, side)
    group = lax.div(c, block)
    outer = (plane == 0) | (plane == 3)
    helper = (plane == 1) | (plane == 2)
    across = lax.rem(c + block, cols)
    even = lax.rem(r, 2) == 0
    has_west, has_east = c > 0, c < cols - 1
    turn_west = (spot == 0) & has_west
    turn_east = (spot == side - 1) & has_east
    carry_west = (spot == side - 1) & (plane > 0)
    carry_east = (spot == 0) & (plane < 3)
    pass_west = (spot > 0) & (plane > 0)
    pass_east = (spot < side - 1) & (plane < 3)
    west_end, east_end = plane * side - 1, (plane + 1) * side

    def remote(src, dst, index, device, sender=None):
        return pltpu.make_async_remote_copy(
            src_ref=src, dst_ref=dst,
            send_sem=pair_send.at[index if sender is None else sender], recv_sem=pair_recv.at[index],
            device_id=device, device_id_type=MESH,
        )

    def when(condition, *actions):
        @pl.when(condition)
        def _():
            for action in actions:
                action()

    def scatter(src, dst, send_sem, recv_sem, peer):
        return pltpu.make_async_remote_copy(
            src_ref=src, dst_ref=dst, send_sem=send_sem, recv_sem=recv_sem,
            device_id={"col": peer}, device_id_type=MESH,
        )

    def everyone(body):
        def step(k, carry):
            body(lax.rem(c + k, cols))
            return carry

        lax.fori_loop(1, cols, step, 0)

    def half_of(index, start, body):
        def step(k, carry):
            body(index * block + lax.rem(c + k, block))
            return carry

        lax.fori_loop(start, block, step, 0)

    def arrived(buffer, sem):
        pltpu.make_async_copy(buffer, buffer, sem).wait()

    barrier = pltpu.get_barrier_semaphore()
    everyone(lambda peer: pl.semaphore_signal(barrier, inc=1, device_id={"col": peer}, device_id_type=MESH))
    for peer in (north, south):
        pl.semaphore_signal(barrier, inc=1, device_id={"row": peer}, device_id_type=MESH)

    pl.semaphore_signal(barrier, inc=1, device_id={"row": south, "col": across}, device_id_type=MESH)
    pairs = [
        (coeffs_hbm, coeffs_ref), (region_hbm, region_ref), (modes_hbm, modes_ref), (object_hbm, object_ref),
        (offsets_hbm, offsets_ref), (counts_hbm, counts_ref), (inten_hbm, inten), (m_hbm, m_ref), (mt_hbm, mt_ref),
    ]
    loads = [pltpu.make_async_copy(src, dst, local_sem.at[i]) for i, (src, dst) in enumerate(pairs)]
    for load in loads:
        load.start()
    for load in loads[:2]:
        load.wait()
    mixes[c] = jnp.zeros((SLOT_ROWS, PAD), F32)
    for p in range(slots):
        weights = coeffs_ref[0, 0, p : p + 1, :]
        area = region_ref[0, :, p : p + 1]
        mixes[c, p : p + 1, :num_modes] = jnp.where(area == r, weights, 0.0)
        mixes[c, p : p + 1, num_modes : 2 * num_modes] = jnp.where(area == r + 1, weights, 0.0)
    for load in loads[2:4]:
        load.wait()
    ext[:, inner, inner] = object_ref[...].astype(BF16)
    pl.semaphore_wait(barrier, cols + 2)

    everyone(lambda peer: scatter(mixes.at[c], mixes.at[c], mix_send, mix_recv, peer).start())
    send_modes = remote(modes_ref, nxt, 0, {"row": north})
    help_modes = remote(modes_ref, help_own, 14, {"row": r, "col": across})
    help_next = remote(modes_ref, help_nxt, 15, {"row": north, "col": across})
    help_pass = remote(help_own, help_nxt, 15, {"row": north})
    when(outer, help_modes.start)
    send_modes.start()
    when(outer & even, help_next.start)
    to_north = remote(ext.at[:, low, inner], ext.at[:, last, inner], 1, {"row": north})
    to_south = remote(ext.at[:, high, inner], ext.at[:, first, inner], 2, {"row": south})
    to_west = remote(ext.at[:, inner, low], ext.at[:, inner, last], 3, {"col": west})
    to_east = remote(ext.at[:, inner, high], ext.at[:, inner, first], 4, {"col": east})
    west_turn = remote(ext.at[:, inner, low], carried.at[0], 16, {"col": c + side - 1})
    east_turn = remote(ext.at[:, inner, high], carried.at[1], 17, {"col": c - side + 1})
    west_pass = remote(carried.at[0], ext.at[:, inner, last], 3, {"col": c - side}, 18)
    east_pass = remote(carried.at[1], ext.at[:, inner, first], 4, {"col": c + side}, 19)
    go_west, go_east = has_west & (spot > 0), has_east & (spot < side - 1)
    when(turn_west, west_turn.start)
    when(turn_east, east_turn.start)
    to_north.start()
    to_south.start()
    when(go_west, to_west.start)
    when(go_east, to_east.start)

    def stack_modes(stack, modes, start):
        for part in range(2):
            stack[start : start + split, pl.ds(part * size, size)] = modes[0, :, part].reshape(split, size)

    stack_modes(stack, modes_ref, 0)
    stack[split:] = jnp.zeros((split, full), BF16)
    help_stack[split:] = jnp.zeros((split, full), BF16)

    arrived(mixes.at[others], mix_recv)
    mixed = mixes[...].reshape(cols * SLOT_ROWS, PAD)
    coarse = mixed.astype(BF16)
    fine = (mixed - coarse.astype(F32)).astype(BF16)
    repeat = where_bf16(iota((PAD, width), 0) == lax.div(iota((PAD, width), 1), strip))
    diagonal = iota((strip, width), 0) == lax.rem(iota((strip, width), 1), strip)
    for i, part in enumerate((coarse, fine)):
        wide = dot(part, repeat).reshape(cols, SLOT_ROWS, width)
        for p in range(slots):
            spread = jnp.where(diagonal[None], wide[:, p : p + 1, :], 0.0)
            kron[i, p] = spread.reshape(size, width).astype(BF16)

    def probe_copy(share, p, index, strip_index, peer):
        return scatter(share.at[p, index], probes.at[p, strip_index], probe_send.at[p], probe_recv.at[p], peer)

    def mix_slot(p):
        both = dot(kron[0, p], stack[...]) + dot(kron[1, p], stack[...])
        for part in range(2):
            value = both[:, part * size : (part + 1) * size].astype(BF16)
            share[p, :, part] = value.reshape(cols, strip, size)
        when(helper, lambda: half_of(1 - group, 0, lambda peer: probe_copy(share, p, peer, c, peer).start()))
        half_of(group, 1, lambda peer: probe_copy(share, p, peer, c, peer).start())
        probes[p, c] = share[p, c]

    def help_slot(p):
        @pl.when(helper)
        def _():
            lines = pl.ds(pl.multiple_of(group * half, half), half)
            both = dot(kron[0, p, lines], help_stack[...]) + dot(kron[1, p, lines], help_stack[...])
            for part in range(2):
                value = both[:, part * size : (part + 1) * size].astype(BF16)
                help_share[p, :, part] = value.reshape(block, strip, size)
            half_of(group, 1, lambda peer: probe_copy(help_share, p, lax.rem(peer, block), across, peer).start())
            probes[p, across] = help_share[p, lax.rem(c, block)]

    mix_slot(0)

    @pl.when(helper)
    def _():
        help_modes.wait_recv()
        when(jnp.logical_not(even), help_pass.start)
        stack_modes(help_stack, help_own, 0)

    help_slot(0)
    when(carry_west, west_turn.wait_recv, west_pass.start)
    when(carry_east, east_turn.wait_recv, east_pass.start)
    to_south.wait_recv()
    north_west = remote(ext.at[:, first, low], ext.at[:, first, last], 5, {"col": west})
    north_east = remote(ext.at[:, first, high], ext.at[:, first, first], 6, {"col": east})
    when(has_west, north_west.start)
    when(has_east, north_east.start)
    to_north.wait_recv()
    south_west = remote(ext.at[:, last, low], ext.at[:, last, last], 7, {"col": west})
    south_east = remote(ext.at[:, last, high], ext.at[:, last, first], 8, {"col": east})
    when(has_west, south_west.start)
    when(has_east, south_east.start)
    send_modes.wait_recv()
    stack_modes(stack, nxt, split)
    mix_slot(1)

    @pl.when(helper)
    def _():
        help_next.wait_recv()
        stack_modes(help_stack, help_nxt, split)

    help_slot(1)
    for p in range(2, slots):
        mix_slot(p)
        help_slot(p)

    repeat_t = where_bf16(iota((width, PAD), 1) == lax.div(iota((width, PAD), 0), strip))
    diagonal_t = lax.rem(iota((width, size), 0), strip) == lax.rem(iota((width, size), 1), strip)
    for i, part in enumerate((coarse, fine)):
        wide_t = lax.dot_general(repeat_t, part, (((1,), (1,)), ((), ())), preferred_element_type=F32).astype(BF16)
        for p in range(slots):
            sel_shape = (cols * SLOT_ROWS, size)
            select = where_bf16(iota(sel_shape, 0) == lax.div(iota(sel_shape, 1), strip) * SLOT_ROWS + p)
            kron_t[i, p] = jnp.where(diagonal_t, dot(wide_t, select), 0.0).astype(BF16)
    acc[...] = jnp.zeros_like(acc)
    for load in loads[4:]:
        load.wait()

    when(has_east, *(copy.wait_recv for copy in (to_west, north_west, south_west)))
    when(has_west, *(copy.wait_recv for copy in (to_east, north_east, south_east)))
    for copy in (to_north, to_south):
        copy.wait_send()
    when(go_west, to_west.wait_send)
    when(go_east, to_east.wait_send)
    when(turn_west, west_turn.wait_send)
    when(turn_east, east_turn.wait_send)
    when(has_west, north_west.wait_send, south_west.wait_send)
    when(has_east, north_east.wait_send, south_east.wait_send)
    for edge, box in (
        (r == 0, (slice(None), first, slice(None))),
        (r == rows - 1, (slice(None), last, slice(None))),
        (c == 0, (slice(None), pl.ds(0, full), first)),
        (c == cols - 1, (slice(None), pl.ds(0, full), last)),
    ):

        @pl.when(edge)
        def _(box=box):
            ext[box] = jnp.zeros_like(ext[box])

    def corner(p, axis):
        return offsets_ref[0, 0, axis : axis + 1, p : p + 1] + half

    for p in range(slots):
        pick_rows = where_bf16(iota((size, full), 1) == iota((size, full), 0) + corner(p, 0))
        pick_cols = where_bf16(iota((full, size), 0) == iota((full, size), 1) + corner(p, 1))
        for plane in range(2):
            narrow = dot(ext[plane], pick_cols).astype(BF16)
            windows[p, plane] = dot(pick_rows, narrow).astype(BF16)

    def send_terms(p):
        everyone(
            lambda peer: scatter(terms.at[p, peer], got_terms.at[p, c], term_send.at[p], term_recv.at[p], peer).start()
        )
        got_terms[p, c] = terms[p, c]

    def position(p):
        when(outer, lambda: arrived(probes.at[p, others], probe_recv.at[p]))
        when(helper, lambda: arrived(probes.at[p, pl.ds(0, cols - 2)], probe_recv.at[p]))
        pr_re = probes[p, :, 0].reshape(size, size).astype(F32)
        pr_im = probes[p, :, 1].reshape(size, size).astype(F32)
        w_re = windows[p, 0].astype(F32)
        w_im = windows[p, 1].astype(F32)
        e_re = (pr_re * w_re - pr_im * w_im).astype(BF16)
        e_im = (pr_re * w_im + pr_im * w_re).astype(BF16)
        left = dot(m_ref[...], jnp.concatenate([e_re, e_im], axis=0)).astype(BF16)
        far = dot(jnp.concatenate([left[:size], left[size:]], axis=1), mt_ref[...])
        f_re, f_im = far[:, :size], far[:, size:]
        energy = jnp.maximum(f_re * f_re + f_im * f_im, FLOOR * FLOOR)
        live = jnp.where(counts_ref[...] > p, 1.0, 0.0)
        factor = (jnp.sqrt(inten[0, 0, p].astype(F32)) * lax.rsqrt(energy) - 1.0) * live
        c_re = (f_re * factor).astype(BF16)
        c_im = (f_im * factor).astype(BF16)
        back = dot(mt_ref[...], jnp.concatenate([c_re, c_im], axis=0)).astype(BF16)
        update = dot(jnp.concatenate([back[:size], back[size:]], axis=1), m_ref[...])
        u_re, u_im = update[:, :size], update[:, size:]
        terms[p, :, 0] = (w_re * u_re + w_im * u_im).astype(BF16).reshape(cols, strip, size)
        terms[p, :, 1] = (w_re * u_im - w_im * u_re).astype(BF16).reshape(cols, strip, size)
        if p < slots - 1:
            send_terms(p)
        put_rows = where_bf16(iota((full, size), 0) == iota((full, size), 1) + corner(p, 0))
        put_cols = where_bf16(iota((size, full), 1) == iota((size, full), 0) + corner(p, 1))
        for plane, value in enumerate((pr_re * u_re + pr_im * u_im, pr_re * u_im - pr_im * u_re)):
            acc[plane] += dot(put_rows, dot(value.astype(BF16), put_cols).astype(BF16))

    for p in range(slots):
        position(p)

    out_cols[0] = acc[:, :, first].astype(BF16)
    out_cols[1] = acc[:, :, last].astype(BF16)
    quarter = full // 4

    def piece(buffer, side_of, i):
        return buffer.at[side_of, :, pl.ds(pl.multiple_of(i * quarter, quarter), quarter)]

    cols_west = remote(out_cols.at[0], got_cols.at[1], 9, {"col": west})
    cols_east = remote(out_cols.at[1], got_cols.at[0], 10, {"col": east})
    west_parts = [remote(piece(out_cols, 0, i), piece(got_cols, 1, i), 26 + i, {"col": west}) for i in range(4)]
    east_parts = [remote(piece(out_cols, 1, i), piece(got_cols, 0, i), 30 + i, {"col": east}) for i in range(4)]
    west_turns = [remote(piece(out_cols, 0, i), carried_out.at[0], 22, {"col": c + i}, 34 + i) for i in range(1, 4)]
    east_turns = [remote(piece(out_cols, 1, i), carried_out.at[1], 23, {"col": c - 3 + i}, 38 + i) for i in range(3)]
    west_pass_out = remote(carried_out.at[0], piece(got_cols, 1, spot), 26 + spot, {"col": west_end}, 24)
    east_pass_out = remote(carried_out.at[1], piece(got_cols, 0, spot), 30 + spot, {"col": east_end}, 25)
    when(turn_west, *(copy.start for copy in west_turns), west_parts[0].start)
    when(turn_east, *(copy.start for copy in east_turns), east_parts[3].start)
    when(go_west, cols_west.start)
    when(go_east, cols_east.start)
    send_terms(slots - 1)

    def gather(p, part_of):
        both = jnp.concatenate([got_terms[p, :, plane].reshape(size, size) for plane in range(2)], axis=1)
        where = pl.ds(part_of * split, split)
        value = dot(kron_t[0, p, where], both) + dot(kron_t[1, p, where], both)
        if p == 0:
            sums[where] = value
        else:
            sums[where] += value

    arrived(got_terms.at[0, others], term_recv.at[0])
    gather(0, 1)
    when(pass_west, west_turns[0].wait_recv, west_pass_out.start)
    when(pass_east, east_turns[0].wait_recv, east_pass_out.start)
    for p in range(1, slots - 2):
        arrived(got_terms.at[p, others], term_recv.at[p])
        gather(p, 1)

    when(go_west, cols_east.wait_recv)
    when(turn_west, *(copy.wait_recv for copy in east_parts))
    acc[:, :, low] += jnp.where(c == 0, 0.0, got_cols[0].astype(F32))
    when(go_east, cols_west.wait_recv)
    when(turn_east, *(copy.wait_recv for copy in west_parts))
    acc[:, :, high] += jnp.where(c == cols - 1, 0.0, got_cols[1].astype(F32))
    out_rows[0] = acc[:, first, inner].astype(BF16)
    out_rows[1] = acc[:, last, inner].astype(BF16)
    rows_north = remote(out_rows.at[0], got_rows.at[1], 11, {"row": north})
    rows_south = remote(out_rows.at[1], got_rows.at[0], 12, {"row": south})
    rows_north.start()
    rows_south.start()

    for p in range(slots - 2, slots):
        arrived(got_terms.at[p, others], term_recv.at[p])
        gather(p, 1)
    for plane in range(2):
        part = sums[split:, pl.ds(plane * size, size)].astype(BF16)
        out_sums[:, plane] = part.reshape(num_modes, strip, size)
    send_sums = remote(out_sums, got_sums, 13, {"row": south})
    send_sums.start()
    for p in range(slots):
        gather(p, 0)

    rows_south.wait_recv()
    grad_ref[:, pl.ds(0, half), :] = acc[:, low, inner] + jnp.where(r == 0, 0.0, got_rows[0].astype(F32))
    rows_north.wait_recv()
    grad_ref[:, pl.ds(half, half), :] = acc[:, high, inner] + jnp.where(r == rows - 1, 0.0, got_rows[1].astype(F32))
    send_sums.wait_recv()
    for plane in range(2):
        own = sums[:split, pl.ds(plane * size, size)].reshape(num_modes, strip, size)
        mode_ref[0, :, plane] = own + got_sums[:, plane].astype(F32)

    for copy in (send_modes, rows_north, rows_south, send_sums):
        copy.wait_send()
    when(outer, help_modes.wait_send)
    when(outer & even, help_next.wait_send)
    when(helper & jnp.logical_not(even), help_pass.wait_send)
    when(carry_west, west_pass.wait_send)
    when(carry_east, east_pass.wait_send)
    when(pass_west, west_pass_out.wait_send)
    when(pass_east, east_pass_out.wait_send)
    when(turn_west, *(copy.wait_send for copy in west_turns), west_parts[0].wait_send)
    when(turn_east, *(copy.wait_send for copy in east_turns), east_parts[3].wait_send)
    when(go_west, cols_west.wait_send)
    when(go_east, cols_east.wait_send)
    arrived(mixes.at[others], mix_send)
    for p in range(slots):
        near = pl.ds(0, block - 1)
        arrived(share.at[p, near], probe_send.at[p])
        when(helper, lambda p=p: arrived(share.at[p, pl.ds(0, block)], probe_send.at[p]))
        when(helper, lambda p=p: arrived(help_share.at[p, near], probe_send.at[p]))
        arrived(terms.at[p, others], term_send.at[p])


def local(object_field, modes, coeffs, offsets, region, counts, intensity):
    size = modes.shape[-1]
    half = size // 2
    full = 2 * size
    num_modes = modes.shape[1]
    slots = coeffs.shape[2]
    strip = modes.shape[3]
    rows, cols = lax.axis_size("row"), lax.axis_size("col")
    block, block_t = dft_blocks(size)
    width = 2 * num_modes * strip
    vmem = pl.BlockSpec(memory_space=pltpu.VMEM)
    hbm = pl.BlockSpec(memory_space=pl.ANY)
    pieces = (slots, cols, 2, strip, size)
    dma = pltpu.SemaphoreType.DMA
    args = (
        object_field, modes, coeffs, jnp.swapaxes(offsets, 2, 3), region, counts, intensity, jnp.asarray(block), jnp.asarray(block_t),
    )
    return pl.pallas_call(
        functools.partial(kernel, (rows, cols, slots, num_modes, strip)),
        out_shape=(
            pltpu.VMEM((2, size, size), F32),
            pltpu.VMEM((1, num_modes, 2, strip, size), F32),
        ),
        in_specs=[hbm] * len(args),
        out_specs=(vmem, vmem),
        scratch_shapes=[pltpu.VMEM(x.shape, x.dtype) for x in args]
        + [
            pltpu.VMEM((2, full, full), BF16),
            pltpu.VMEM(modes.shape, BF16),
            pltpu.VMEM((cols, SLOT_ROWS, PAD), F32),
            pltpu.VMEM((width, full), BF16),
            pltpu.VMEM((2, slots, size, width), BF16),
            pltpu.VMEM((2, slots, width, size), BF16),
            pltpu.VMEM(pieces, BF16),
            pltpu.VMEM(pieces, BF16),
            pltpu.VMEM((slots, 2, size, size), BF16),
            pltpu.VMEM(modes.shape, BF16),
            pltpu.VMEM(modes.shape, BF16),
            pltpu.VMEM((width, full), BF16),
            pltpu.VMEM((slots, cols // 2, 2, strip, size), BF16),
            pltpu.VMEM((2, 2, size, half), BF16),
            pltpu.VMEM((2, 2, full // 4, half), BF16),
            pltpu.VMEM(pieces, BF16),
            pltpu.VMEM(pieces, BF16),
            pltpu.VMEM((2, full, full), F32),
            pltpu.VMEM((2, 2, full, half), BF16),
            pltpu.VMEM((2, 2, full, half), BF16),
            pltpu.VMEM((2, 2, half, size), BF16),
            pltpu.VMEM((2, 2, half, size), BF16),
            pltpu.VMEM((width, full), F32),
            pltpu.VMEM((num_modes, 2, strip, size), BF16),
            pltpu.VMEM((num_modes, 2, strip, size), BF16),
            dma((len(args),)),
            dma((42,)),
            dma((42,)),
            dma,
            dma,
            dma((slots,)),
            dma((slots,)),
            dma((slots,)),
            dma((slots,)),
        ],
        compiler_params=pltpu.CompilerParams(
            collective_id=0, has_side_effects=True, vmem_limit_bytes=56 << 20
        ),
        name="ptychography",
    )(*args)


def solution(mesh):
    in_specs = (
        P(None, "row", "col"),
        P("row", None, None, "col", None),
        P("row", "col", None, None),
        P("row", "col", None, None),
        P("row", "col", None),
        P("row", "col"),
        P("row", "col", None, None, None),
    )
    out_specs = (P(None, "row", "col"), P("row", None, None, "col", None))
    return jax.shard_map(local, mesh=mesh, in_specs=in_specs, out_specs=out_specs, check_vma=False)
```
